32 devices in a mesh: lat: 4 (over z), lon: 8 (over y, x, core).
Axes of the slice: x: 2, y: 2, z: 4, core: 2. Of those that a mesh axis runs over, the one named last changes fastest.
Arguments:
- control: float32 [16, 137, 32, 1024], P('lon', None, 'lat'), may hold values from -6 to 6
- ensemble: bfloat16 [16, 137, 32, 1024], P(None, None, 'lat', 'lon'), may hold values from -2.5 to 2.5
- vertical_root: bfloat16 [137, 137], replicated, may hold values from -0.5 to 0.5
- sector_band: bfloat16 [3, 128, 1024], P(None, None, 'lon'), may hold values from -0.3125 to 0.3125
- latitude_taps: float32 [9, 1024], P(None, 'lon'), may hold values from -2 to 2
- innovation: float32 [137, 32, 1024], P(None, 'lat', 'lon'), may hold values from -6 to 6
- inverse_error: float32 [137, 32, 1024], P(None, 'lat', 'lon'), may hold values from 0.5 to 2
Outputs:
- gradient: float32 [16, 137, 32, 1024], P('lon', None, 'lat')
- departure: float32 [137, 32, 1024], P(None, 'lat', 'lon')
The draws below stay inside these ranges and needn't reach their ends.
All inputs are finite; a program needn't handle non-finite values.
Results may differ from the reference program's by a relative error of at most 0.007.
Values may be sent and summed in bfloat16 or wider, within the bound.
A program may use at most 128 MiB of HBM per device.

```python
import math
import jax
import jax.numpy as jnp
from jax import lax

MEMBERS = 16
LEVELS = 137
CX = 128
SPAN = 9
NY = 32
NX = 1024


def block_scale(rng, dims, shards, least, high):
    def one(position, blocks):
        draws = jax.random.uniform(jax.random.fold_in(jax.random.fold_in(rng, 6), position), (blocks,), jnp.float32, least / len(shards), high / len(shards))
        return jnp.repeat(jnp.exp(draws), dims[position] // blocks).reshape((-1,) + (1,) * (len(dims) - position - 1))

    gain = one(*shards[0])
    for cut in shards[1:]:
        gain = gain * one(*cut)
    return gain


def gaussian(rng, shape, scale, bound, shards=(), dtype=jnp.bfloat16):
    drawn = jax.random.normal(rng, shape, jnp.float32) * scale
    if len(shards) > 0:
        drawn = block_scale(rng, shape, shards, -0.22, 0.18) * drawn
    return jnp.clip(drawn, min=-bound, max=bound).astype(dtype)


def setup_inputs(seed: int = 0) -> dict:
    arg_keys = jax.random.split(jax.random.key(seed), 8)
    return {
        "control": gaussian(arg_keys[0], (MEMBERS, LEVELS, NY, NX), 1.0, 6.0, ((0, 8), (2, 4)), jnp.float32),
        "ensemble": gaussian(arg_keys[1], (MEMBERS, LEVELS, NY, NX), 0.35, 2.5, ((2, 4), (3, 8))),
        "vertical_root": gaussian(arg_keys[2], (LEVELS, LEVELS), LEVELS ** -0.5, 0.5),
        "sector_band": gaussian(arg_keys[3], (3, CX, NX), (3 * CX) ** -0.5, 0.3125, ((2, 8),)),
        "latitude_taps": gaussian(arg_keys[4], (SPAN, NX), SPAN ** -0.5, 2.0, ((1, 8),), jnp.float32),
        "innovation": gaussian(arg_keys[5], (LEVELS, NY, NX), 1.0, 6.0, ((1, 4), (2, 8)), jnp.float32),
        "inverse_error": jnp.clip(jnp.exp(math.log(2.0) - 1.3862944 * jax.random.uniform(arg_keys[6], (LEVELS, NY, NX), jnp.float32) ** block_scale(arg_keys[6], (LEVELS, NY, NX), ((1, 4), (2, 8)), -0.2, 0.2)), 0.5, 2.0),
    }


def blocked_band(sector_band):
    taps, width, total = sector_band.shape
    count = total // width
    return sector_band.reshape(taps, width, count, width).transpose(2, 0, 1, 3).reshape(count, taps * width, width)


def reference(control, ensemble, vertical_root, sector_band, latitude_taps, innovation, inverse_error):
    levels, height, total = innovation.shape
    width = sector_band.shape[1]
    count = total // width
    half = latitude_taps.shape[0] // 2
    band_blocks = blocked_band(sector_band).astype(jnp.float32)

    def forward(member):
        coarse = member.astype(jnp.bfloat16)
        mixed = jnp.dot(vertical_root, coarse.reshape(levels, -1), preferred_element_type=jnp.float32)
        mixed = mixed.astype(jnp.bfloat16).reshape(levels, height, count, width)
        stacked = jnp.concatenate([jnp.roll(mixed, 1, axis=2), mixed, jnp.roll(mixed, -1, axis=2)], axis=3)
        spread = jnp.einsum('lybk,bkj->lybj', stacked.astype(jnp.float32), band_blocks)
        spread = lax.optimization_barrier(spread.astype(jnp.bfloat16)).reshape(levels, height, total)
        padded = jnp.pad(spread.astype(jnp.float32), ((0, 0), (half, half), (0, 0)))
        stencil = jnp.zeros((levels, height, total), jnp.float32)
        for offset in range(-half, half + 1):
            stencil = stencil + latitude_taps[offset + half][None, None, :] * padded[:, half + offset:half + offset + height, :]
        return stencil

    def accumulate(running, pair):
        member, perturb = pair
        return running + perturb.astype(jnp.float32) * forward(member), None

    increment, _ = lax.scan(accumulate, jnp.zeros((levels, height, total), jnp.float32), (control, ensemble))
    departure = inverse_error * (increment - innovation)

    def backward(pair):
        member, perturb = pair
        pulled = lax.optimization_barrier((perturb.astype(jnp.float32) * departure).astype(jnp.bfloat16))
        padded = jnp.pad(pulled.astype(jnp.float32), ((0, 0), (half, half), (0, 0)))
        spread_back = jnp.zeros((levels, height, total), jnp.float32)
        for offset in range(-half, half + 1):
            spread_back = spread_back + latitude_taps[offset + half][None, None, :] * padded[:, half - offset:half - offset + height, :]
        spread_back = spread_back.astype(jnp.bfloat16).reshape(levels, height, count, width)
        terms = jnp.einsum('lybj,bkj->lybk', spread_back.astype(jnp.float32), band_blocks)
        terms = lax.optimization_barrier(terms.astype(jnp.bfloat16)).astype(jnp.float32)
        summed = terms[..., width:2 * width] + jnp.roll(terms[..., 2 * width:], 1, axis=2) + jnp.roll(terms[..., :width], -1, axis=2)
        summed = summed.astype(jnp.bfloat16).reshape(levels, -1)
        returned = jnp.dot(vertical_root.T, summed, preferred_element_type=jnp.float32).astype(jnp.bfloat16)
        return member + returned.reshape(levels, height, total).astype(jnp.float32)

    gradient = lax.map(backward, (control, ensemble))
    return gradient, departure
```

```python
import functools

import jax
import jax.numpy as jnp
from jax import lax
from jax.experimental import pallas as pl
from jax.experimental.pallas import tpu as pltpu
from jax.sharding import PartitionSpec as P

F32, BF16 = jnp.float32, jnp.bfloat16
VMEM_LIMIT = 62 * 1024 * 1024
GROUP = 16
OFFSETS = (1, 3, 4, 7, 8, 9, 10)
MESH = pl.DeviceIdType.MESH


def lanes(block, width):
    return pl.ds(pl.multiple_of(block * width, width), width)


def loop(start, stop, body, unroll=1):
    def step(i, _):
        body(i)
        return 0

    lax.fori_loop(start, stop, step, 0, unroll=unroll)


def program(
    control, ensemble, root, band, taps, innovation, inverse,
    summed, departure,
    held, raw, turn, packed, own_e, below_e, above_e, spread, fields,
    sums, mate_sums, below_sums, above_sums, chip_sums, facts,
    inn, inv, bands, all_taps,
    held_sems, raw_sems, fact_load_sems, out_sems, dep_sem,
    e_sems, up_sems, down_sems, core_sems, sum_sems, chip_sems, spread_sems,
    fact_sems, mate_sems, band_sems, band_mate_sems, tap_sems,
):
    blocks, own, height, padded, width = packed.shape
    levels, members = root.shape[0], blocks * own
    rows = levels * height
    half = taps.shape[0] // 2
    extended = height + 2 * half
    chips = blocks // 2
    chunks = padded // GROUP
    together = 3 if chunks % 3 == 0 else 1
    tail = levels - (chunks - 1) * GROUP
    me, row = lax.axis_index("lon"), lax.axis_index("lat")
    core = lax.rem(me, 2)
    chip = lax.div(me, 2)
    mate = me + 1 - 2 * core
    has_below, has_above = row > 0, row < lax.axis_size("lat") - 1

    def at_levels(c):
        return pl.ds(pl.multiple_of(c * GROUP, GROUP), GROUP)

    def remote(source, target, sems, sent, landed, **device):
        return pltpu.make_async_remote_copy(
            src_ref=source, dst_ref=target, send_sem=sems.at[(0,) + sent],
            recv_sem=sems.at[(1,) + landed], device_id=device, device_id_type=MESH,
        )

    def when(guard, action):
        @pl.when(guard)
        def _():
            action()

    def load_control(k, b):
        return pltpu.make_async_copy(
            control.at[k, :, lanes(b, width)], held.at[b, pl.ds(0, rows)], held_sems.at[b]
        )

    def load_raw(c, act):
        @pl.when(c < chunks - 1)
        def _():
            act(pltpu.make_async_copy(
                ensemble.at[:, at_levels(c)], raw.at[:, at_levels(c)], raw_sems.at[c]))

        @pl.when(c == chunks - 1)
        def _():
            last = pl.ds(levels - tail, tail)
            act(pltpu.make_async_copy(
                ensemble.at[:, last], raw.at[:, last], raw_sems.at[c]))

    loop(0, chunks, lambda c: load_raw(c, lambda copy: copy.start()))
    loop(0, blocks, lambda b: load_control(0, b).start())
    load_inn = pltpu.make_async_copy(innovation, inn.at[pl.ds(0, rows)], fact_load_sems.at[0])
    load_inv = pltpu.make_async_copy(inverse, inv.at[pl.ds(0, rows)], fact_load_sems.at[1])
    load_inn.start()
    load_inv.start()

    barrier = pltpu.get_barrier_semaphore()
    loop(1, blocks, lambda t: pl.semaphore_signal(
        barrier, inc=1, device_id={"lon": lax.rem(me + t, blocks)}, device_id_type=MESH))
    when(has_below, lambda: pl.semaphore_signal(
        barrier, inc=1, device_id={"lat": row - 1}, device_id_type=MESH))
    when(has_above, lambda: pl.semaphore_signal(
        barrier, inc=1, device_id={"lat": row + 1}, device_id_type=MESH))
    inner = jnp.logical_and(has_below, has_above)
    when(inner, lambda: pl.semaphore_wait(barrier, blocks + 1))
    when(jnp.logical_not(inner), lambda: pl.semaphore_wait(barrier, blocks))

    def same_core(t):
        return lax.rem(chip + t, chips)

    def band_copy(slot, target):
        return remote(bands.at[slot], bands.at[slot], band_sems, (target,), (slot,), lon=target)

    def band_mate(slot, landed):
        return remote(bands.at[slot], bands.at[slot], band_mate_sems, (slot,), (landed,), lon=mate)

    def tap_copy(slot, target):
        return remote(all_taps.at[slot], all_taps.at[slot], tap_sems, (target,), (slot,), lon=target)

    bands[me] = band[...]
    all_taps[me] = taps[...]
    loop(1, chips, lambda t: band_copy(me, 2 * same_core(t) + core).start())
    band_mate(me, me).start()
    loop(1, blocks, lambda t: tap_copy(me, lax.rem(me + t, blocks)).start())

    def e_copy(c, target, slot):
        return remote(
            packed.at[target, :, :, at_levels(c)], own_e.at[slot, :, :, at_levels(c)],
            e_sems, (c, target), (c, slot), lon=target)

    def up_copy(c, s):
        return remote(
            own_e.at[s, :, pl.ds(height - half, half), at_levels(c)],
            below_e.at[s, :, :, at_levels(c)], up_sems, (c, s), (c, s), lat=row + 1)

    def down_copy(c, s):
        return remote(
            own_e.at[s, :, pl.ds(0, half), at_levels(c)],
            above_e.at[s, :, :, at_levels(c)], down_sems, (c, s), (c, s), lat=row - 1)

    def pass_on(c, s):
        when(has_above, lambda: up_copy(c, s).start())
        when(has_below, lambda: down_copy(c, s).start())

    def repack(place, target, c):
        for k in range(own):
            value = raw[place * own + k, at_levels(c)].astype(F32)
            turn[k] = value.reshape(GROUP * height, width)
            for y in range(height):
                target[k, y, at_levels(c), :] = turn[
                    k, pl.ds(y, GROUP, stride=height), :].astype(BF16)

    def clear_raw(m):
        for l in range(levels, padded):
            raw[m, l] = jnp.zeros((height, width), BF16)

    loop(0, members, clear_raw)

    def send_near(c):
        load_raw(c, lambda copy: copy.wait())
        repack(mate, packed.at[mate], c)
        e_copy(c, mate, me).start()
        repack(me, own_e.at[me], c)
        pass_on(c, me)

    def send_far(c):
        def other(t):
            p = lax.rem(2 * chip + t, blocks)
            repack(p, packed.at[p], c)
            e_copy(c, p, me).start()

        loop(2, blocks, other)

    def relay(c, s):
        e_copy(c, s, s).wait_recv()
        pass_on(c, s)

    def relay_far(c):
        loop(2, blocks, lambda t: relay(c, lax.rem(2 * chip + t, blocks)))

    loop(0, chunks, send_near)
    loop(0, chunks, send_far)
    loop(0, chunks, lambda c: relay(c, mate))

    edge = (blocks, own, half)
    zero_rows = jnp.zeros((padded, width), BF16)

    def clear_edges(target):
        def clear(b):
            for k in range(own):
                for y in range(half):
                    target[b, k, y] = zero_rows

        loop(0, blocks, clear)

    def clear_facts(first):
        def clear(j):
            for parity in range(2):
                for y in range(half):
                    facts[parity, j, first + y] = zero_rows

        loop(0, chips, clear)

    def clear_sums(target):
        def clear(j):
            for y in range(half):
                target[j, y] = zero_rows

        loop(0, chips, clear)

    def clear_below():
        clear_edges(below_e)
        clear_facts(0)
        clear_sums(below_sums)

    def clear_above():
        clear_edges(above_e)
        clear_facts(height + half)
        clear_sums(above_sums)

    when(jnp.logical_not(has_below), clear_below)
    when(jnp.logical_not(has_above), clear_above)
    inn[pl.ds(rows, padded * height - rows), :] = jnp.zeros((padded * height - rows, width), F32)
    inv[pl.ds(rows, padded * height - rows), :] = jnp.zeros((padded * height - rows, width), F32)

    def clear_tail(b):
        for k in range(own):
            for y in range(height):
                fields[k, y, pl.ds(padded - GROUP, GROUP), lanes(b, width)] = jnp.zeros(
                    (GROUP, width), BF16)

    loop(0, blocks, clear_tail)

    for k in range(own):
        if k > 0:
            relay_far(k - 1)

        def vertical(b):
            load_control(k, b).wait()
            columns = jnp.concatenate(
                [held[b, pl.ds(y, levels, stride=height), :] for y in range(height)], axis=1)
            out = jnp.dot(root[...], columns.astype(BF16), preferred_element_type=F32).astype(BF16)
            for y in range(height):
                fields[k, y, pl.ds(0, levels), lanes(b, width)] = out[:, y * width : (y + 1) * width]
            if k + 1 < own:
                load_control(k + 1, b).start()

        loop(0, blocks, vertical)
        if k == 0:
            def forward_band(t):
                s = 2 * same_core(t) + core
                band_copy(s, s).wait_recv()
                band_mate(s, s).start()

            loop(1, chips, forward_band)
            loop(0, chips, lambda j: band_mate(
                2 * j + 1 - core, 2 * j + 1 - core).wait_recv())
            loop(1, blocks, lambda t: tap_copy(
                lax.rem(me + t, blocks), lax.rem(me + t, blocks)).wait_recv())

        def longitude(b):
            parts = [
                fields[k, :, :, lanes(lax.rem(b + blocks + o, blocks), width)] for o in (-1, 0, 1)]
            left = jnp.concatenate([part.reshape(height * padded, width) for part in parts], axis=1)
            out = jnp.dot(left, bands[b], preferred_element_type=F32)
            spread[b, k] = out.astype(BF16).reshape(height, padded, width)

        loop(0, blocks, longitude)

    def tap_rows(s):
        return [
            jnp.broadcast_to(all_taps[s, pl.ds(o, 1), :], (GROUP, width))
            for o in range(2 * half + 1)]

    def e_row(s, k, r, c):
        if r < half:
            value = below_e[s, k, r, at_levels(c), :]
        elif r < half + height:
            value = own_e[s, k, r - half, at_levels(c), :]
        else:
            value = above_e[s, k, r - half - height, at_levels(c), :]
        return value.astype(F32)

    def stencil(s, c, put):
        tap = tap_rows(s)
        field = [
            [spread[s, k, y, at_levels(c), :].astype(F32) for y in range(height)]
            for k in range(own)]
        for r in range(extended):
            total = None
            for k in range(own):
                part = None
                for o in range(-half, half + 1):
                    y = r - half + o
                    if 0 <= y < height:
                        term = tap[o + half] * field[k][y]
                        part = term if part is None else part + term
                part = part * e_row(s, k, r, c)
                total = part if total is None else total + part
            put(r, total)

    def held_row(j, r, c):
        return 2 * j + r // height, pl.ds(
            pl.multiple_of((r % height) * padded + c * GROUP, GROUP), GROUP)

    def get_held(j, r, c):
        b, at = held_row(j, r, c)
        return held[b, at, :]

    def put_held(j, r, c, value):
        b, at = held_row(j, r, c)
        held[b, at, :] = value

    def core_copy(c, j):
        return remote(sums.at[j, :, at_levels(c)], mate_sums.at[j, :, at_levels(c)],
                      core_sems, (c, j), (c, j), lon=mate)

    def forward(c):
        def other(j):
            for parity in range(2):
                when(has_below, lambda: up_copy(c, 2 * j + parity).wait_recv())
                when(has_above, lambda: down_copy(c, 2 * j + parity).wait_recv())

            def put(r, value):
                sums[j, r, at_levels(c), :] = value.astype(BF16)

            stencil(2 * j + 1 - core, c, put)
            core_copy(c, j).start()

        loop(0, chips, other)
        loop(0, chips, lambda j: stencil(
            2 * j + core, c, lambda r, value: put_held(j, r, c, value)))

    def sum_up(c):
        return remote(sums.at[:, pl.ds(half + height, half), at_levels(c)],
                      below_sums.at[:, :, at_levels(c)], sum_sems, (c, 0), (c, 0), lat=row + 1)

    def sum_down(c):
        return remote(sums.at[:, pl.ds(0, half), at_levels(c)],
                      above_sums.at[:, :, at_levels(c)], sum_sems, (c, 1), (c, 1), lat=row - 1)

    def combine(c):
        def each(j):
            core_copy(c, j).wait()
            for r in range(extended):
                value = get_held(j, r, c) + mate_sums[j, r, at_levels(c), :].astype(F32)
                if half <= r < half + height:
                    put_held(j, r, c, value)
                else:
                    sums[j, r, at_levels(c), :] = value.astype(BF16)

        loop(0, chips, each)
        when(has_above, lambda: sum_up(c).start())
        when(has_below, lambda: sum_down(c).start())

    def lat_sum(j, y, c):
        value = get_held(j, half + y, c)
        if y < half:
            value = value + below_sums[j, y, at_levels(c), :].astype(F32)
        if y >= height - half:
            value = value + above_sums[j, y - height + half, at_levels(c), :].astype(F32)
        return value

    def chip_copy(c, target, slot):
        return remote(sums.at[target, pl.ds(half, height), at_levels(c)],
                      chip_sums.at[slot, :, at_levels(c)],
                      chip_sems, (c, target), (c, slot), lon=2 * target + core)

    def scatter(c):
        when(has_below, lambda: sum_up(c).wait_recv())
        when(has_above, lambda: sum_down(c).wait_recv())

        def each(t):
            j = same_core(t)
            for y in range(height):
                sums[j, half + y, at_levels(c), :] = lat_sum(j, y, c).astype(BF16)
            chip_copy(c, j, chip).start()

        loop(1, chips, each)

    def spread_copy(c, target, slot):
        own_rows = facts.at[core, slot, pl.ds(half, height), at_levels(c)]
        return remote(own_rows, own_rows, spread_sems, (c, target), (c, slot),
                      lon=2 * target + core)

    def depart(c):
        loop(1, chips, lambda t: chip_copy(c, same_core(t), same_core(t)).wait_recv())
        for y in range(height):
            value = lat_sum(chip, y, c)
            for t in range(1, chips):
                value = value + chip_sums[same_core(t), y, at_levels(c), :].astype(F32)
            at = pl.ds(c * GROUP * height + y, GROUP, stride=height)
            value = inv[at, :] * (value - inn[at, :])
            inn[at, :] = value
            facts[core, chip, half + y, at_levels(c), :] = value.astype(BF16)
        loop(1, chips, lambda t: spread_copy(c, same_core(t), chip).start())

    def fact_up(c):
        return remote(facts.at[core, :, pl.ds(height, half), at_levels(c)],
                      facts.at[core, :, pl.ds(0, half), at_levels(c)],
                      fact_sems, (c, 0), (c, 0), lat=row + 1)

    def fact_down(c):
        return remote(facts.at[core, :, pl.ds(half, half), at_levels(c)],
                      facts.at[core, :, pl.ds(half + height, half), at_levels(c)],
                      fact_sems, (c, 1), (c, 1), lat=row - 1)

    def mate_copy(c, part, parity):
        first, count = ((half, height), (0, half), (half + height, half))[part]
        piece = facts.at[parity, :, pl.ds(first, count), at_levels(c)]
        return remote(piece, piece, mate_sems, (c, part), (c, part), lon=mate)

    def gather(c):
        loop(1, chips, lambda t: spread_copy(c, same_core(t), same_core(t)).wait_recv())
        when(has_above, lambda: fact_up(c).start())
        when(has_below, lambda: fact_down(c).start())
        mate_copy(c, 0, core).start()

    def gather_edges(c):
        def below():
            fact_up(c).wait_recv()
            mate_copy(c, 1, core).start()

        def above():
            fact_down(c).wait_recv()
            mate_copy(c, 2, core).start()

        when(has_below, below)
        when(has_above, above)

    def out_copy(g):
        span = together * GROUP
        at = pl.ds(pl.multiple_of(g * span, span), span)
        return pltpu.make_async_copy(
            spread.at[:, :, :, at], summed.at[:, :, :, at], out_sems.at[g])

    def adjoint(c):
        mate_copy(c, 0, 1 - core).wait_recv()
        when(has_below, lambda: mate_copy(c, 1, 1 - core).wait_recv())
        when(has_above, lambda: mate_copy(c, 2, 1 - core).wait_recv())

        def each(s):
            tap = tap_rows(s)
            fact = [facts[lax.rem(s, 2), lax.div(s, 2), r, at_levels(c), :].astype(F32)
                    for r in range(extended)]
            for k in range(own):
                pulled = [e_row(s, k, r, c) * fact[r] for r in range(extended)]
                for y in range(height):
                    total = None
                    for o in range(-half, half + 1):
                        term = tap[o + half] * pulled[y - o + half]
                        total = term if total is None else total + term
                    fields[k, y, at_levels(c), lanes(s, width)] = total.astype(BF16)

        loop(0, blocks, each)

        if together == 1:
            adjoint_longitude(c)
        else:
            when(lax.rem(c, together) == together - 1,
                 lambda: adjoint_longitude(lax.div(c, together)))

    def adjoint_longitude(g):
        span = together * GROUP
        at = pl.ds(pl.multiple_of(g * span, span), span)

        def longitude(b):
            before, after = lax.rem(b + blocks - 1, blocks), lax.rem(b + 1, blocks)
            right = jnp.concatenate(
                [
                    bands[before, 2 * width : 3 * width],
                    bands[b, width : 2 * width],
                    bands[after, 0:width],
                ],
                axis=0,
            )
            left = jnp.concatenate(
                [
                    jnp.concatenate(
                        [fields[k, :, at, lanes(s, width)].reshape(height * span, width)
                         for k in range(own)], axis=0)
                    for s in (before, b, after)
                ],
                axis=1,
            )
            out = jnp.dot(left, right, preferred_element_type=F32).astype(BF16)
            spread[b, :, :, at, :] = out.reshape(own, height, span, width)

        loop(0, blocks, longitude)
        out_copy(g).start()

    def transpose_bands(b):
        for part in range(3):
            at = slice(part * width, (part + 1) * width)
            bands[b, at] = bands[b, at].astype(F32).T.astype(BF16)

    loop(1, chips, lambda t: band_copy(me, 2 * same_core(t) + core).wait_send())
    loop(0, chips, lambda j: band_mate(2 * j + core, 2 * j + core).wait_send())
    loop(0, blocks, transpose_bands)
    load_inn.wait()
    load_inv.wait()

    def stage(action, c):
        when(jnp.logical_and(c >= 0, c < chunks), lambda: action(c))

    def step(i):
        when(i < chunks, lambda: relay_far(i))
        stage(forward, i - OFFSETS[0])
        stage(combine, i - OFFSETS[1])
        stage(scatter, i - OFFSETS[2])
        stage(depart, i - OFFSETS[3])
        stage(gather, i - OFFSETS[4])
        stage(gather_edges, i - OFFSETS[5])
        stage(adjoint, i - OFFSETS[6])

    loop(own - 1, chunks + OFFSETS[6], step)
    store = pltpu.make_async_copy(inn.at[pl.ds(0, rows)], departure, dep_sem)
    store.start()

    def sent(c):
        loop(1, blocks, lambda t: e_copy(c, lax.rem(me + t, blocks), me).wait_send())
        loop(1, chips, lambda t: chip_copy(c, same_core(t), chip).wait_send())
        loop(1, chips, lambda t: spread_copy(c, same_core(t), chip).wait_send())
        mate_copy(c, 0, core).wait_send()

        def below():
            loop(0, blocks, lambda s: down_copy(c, s).wait_send())
            sum_down(c).wait_send()
            fact_down(c).wait_send()
            mate_copy(c, 1, core).wait_send()

        def above():
            loop(0, blocks, lambda s: up_copy(c, s).wait_send())
            sum_up(c).wait_send()
            fact_up(c).wait_send()
            mate_copy(c, 2, core).wait_send()

        when(has_below, below)
        when(has_above, above)

    loop(0, chunks // together, lambda g: out_copy(g).wait())
    loop(0, chunks, sent)
    loop(1, blocks, lambda t: tap_copy(me, lax.rem(me + t, blocks)).wait_send())
    store.wait()


def finish(control, summed, root, gradient):
    levels = root.shape[0]
    _, _, height, _, width = summed.shape
    right = jnp.concatenate([summed[0, 0, y, 0:levels, :] for y in range(height)], axis=1)
    out = lax.dot_general(
        root[...], right, (((0,), (0,)), ((), ())), preferred_element_type=F32)
    out = out.astype(BF16).astype(F32)
    for y in range(height):
        at = pl.ds(y, levels, stride=height)
        gradient[0, at, :] = control[0, at, :] + out[:, y * width : (y + 1) * width]


def shards(control, ensemble, vertical_root, sector_band, latitude_taps, innovation, inverse_error):
    spans = latitude_taps.shape[0]
    half = spans // 2
    width = sector_band.shape[1]
    own, levels, height, total = control.shape
    members = ensemble.shape[0]
    blocks = total // width
    chips = blocks // 2
    chunks = -(-levels // GROUP)
    padded = chunks * GROUP
    rows = levels * height
    extended = height + 2 * half
    fields = control.reshape(own, rows, total)
    band = sector_band.reshape(3 * width, width)
    dma = pltpu.SemaphoreType.DMA
    vmem = pltpu.VMEM
    local = pl.BlockSpec(memory_space=pltpu.VMEM)
    anywhere = pl.BlockSpec(memory_space=pl.ANY)
    whole = (blocks, own, height, padded, width)
    edges = (blocks, own, half, padded, width)
    summed, departure = pl.pallas_call(
        program,
        in_specs=[anywhere, anywhere, local, local, local, anywhere, anywhere],
        out_specs=[anywhere, anywhere],
        out_shape=[
            jax.ShapeDtypeStruct(whole, BF16),
            jax.ShapeDtypeStruct((rows, width), F32),
        ],
        scratch_shapes=[
            vmem((blocks, height * padded, width), F32),
            vmem((members, padded, height, width), BF16),
            vmem((own, GROUP * height, width), F32),
            vmem(whole, BF16),
            vmem(whole, BF16),
            vmem(edges, BF16),
            vmem(edges, BF16),
            vmem(whole, BF16),
            vmem((own, height, padded, total), BF16),
            vmem((chips, extended, padded, width), BF16),
            vmem((chips, extended, padded, width), BF16),
            vmem((chips, half, padded, width), BF16),
            vmem((chips, half, padded, width), BF16),
            vmem((chips, height, padded, width), BF16),
            vmem((2, chips, extended, padded, width), BF16),
            vmem((padded * height, width), F32),
            vmem((padded * height, width), F32),
            vmem((blocks, 3 * width, width), BF16),
            vmem((blocks, spans, width), F32),
            dma((blocks,)),
            dma((chunks,)),
            dma((2,)),
            dma((chunks,)),
            dma,
            dma((2, chunks, blocks)),
            dma((2, chunks, blocks)),
            dma((2, chunks, blocks)),
            dma((2, chunks, chips)),
            dma((2, chunks, 2)),
            dma((2, chunks, chips)),
            dma((2, chunks, chips)),
            dma((2, chunks, 2)),
            dma((2, chunks, 3)),
            dma((2, blocks)),
            dma((2, blocks)),
            dma((2, blocks)),
        ],
        compiler_params=pltpu.CompilerParams(
            vmem_limit_bytes=VMEM_LIMIT, collective_id=0, has_side_effects=True
        ),
        name="exchange",
    )(fields, ensemble, vertical_root, band, latitude_taps,
      innovation.reshape(rows, width), inverse_error.reshape(rows, width))
    gradient = pl.pallas_call(
        finish,
        grid=(own, blocks),
        in_specs=[
            pl.BlockSpec((1, rows, width), lambda k, b: (k, 0, b)),
            pl.BlockSpec((1, 1, height, padded, width), lambda k, b: (b, k, 0, 0, 0)),
            pl.BlockSpec((levels, levels), lambda k, b: (0, 0)),
        ],
        out_specs=pl.BlockSpec((1, rows, width), lambda k, b: (k, 0, b)),
        out_shape=jax.ShapeDtypeStruct((own, rows, total), F32),
        compiler_params=pltpu.CompilerParams(vmem_limit_bytes=VMEM_LIMIT),
        name="finish",
    )(fields, summed, vertical_root)
    return gradient.reshape(control.shape), departure.reshape(innovation.shape)


def solution(mesh):
    placed = (
        P("lon", None, "lat", None),
        P(None, None, "lat", "lon"),
        P(),
        P(None, None, "lon"),
        P(None, "lon"),
        P(None, "lat", "lon"),
        P(None, "lat", "lon"),
    )
    return jax.shard_map(
        shards,
        mesh=mesh,
        in_specs=placed,
        out_specs=(P("lon", None, "lat", None), P(None, "lat", "lon")),
        check_vma=False,
    )
```

```python
import functools

import jax
import jax.numpy as jnp
from jax import lax
from jax.experimental import pallas as pl
from jax.experimental.pallas import tpu as pltpu
from jax.sharding import PartitionSpec as P

F32, BF16 = jnp.float32, jnp.bfloat16
VMEM_LIMIT = 62 * 1024 * 1024
GROUP = 16
OFFSETS = (1, 3, 4, 7, 8, 9, 10)
MESH = pl.DeviceIdType.MESH


def lanes(block, width):
    return pl.ds(pl.multiple_of(block * width, width), width)


def loop(start, stop, body, unroll=1):
    def step(i, _):
        body(i)
        return 0

    lax.fori_loop(start, stop, step, 0, unroll=unroll)


def program(
    control, ensemble, root, band, taps, innovation, inverse,
    summed, departure,
    held, raw, turn, packed, own_e, below_e, above_e, spread, fields,
    sums, mate_sums, below_sums, above_sums, chip_sums, facts,
    inn, inv, bands, all_taps,
    held_sems, raw_sems, fact_load_sems, out_sems, dep_sem,
    e_sems, up_sems, down_sems, core_sems, sum_sems, chip_sems, spread_sems,
    fact_sems, mate_sems, band_sems, band_mate_sems, tap_sems,
):
    blocks, own, height, padded, width = packed.shape
    levels, members = root.shape[0], blocks * own
    rows = levels * height
    half = taps.shape[0] // 2
    extended = height + 2 * half
    chips = blocks // 2
    chunks = padded // GROUP
    together = 3 if chunks % 3 == 0 else 1
    tail = levels - (chunks - 1) * GROUP
    me, row = lax.axis_index("lon"), lax.axis_index("lat")
    core = lax.rem(me, 2)
    chip = lax.div(me, 2)
    mate = me + 1 - 2 * core
    has_below, has_above = row > 0, row < lax.axis_size("lat") - 1

    def at_levels(c):
        return pl.ds(pl.multiple_of(c * GROUP, GROUP), GROUP)

    def remote(source, target, sems, sent, landed, **device):
        return pltpu.make_async_remote_copy(
            src_ref=source, dst_ref=target, send_sem=sems.at[(0,) + sent],
            recv_sem=sems.at[(1,) + landed], device_id=device, device_id_type=MESH,
        )

    def when(guard, action):
        @pl.when(guard)
        def _():
            action()

    def load_control(k, b):
        return pltpu.make_async_copy(
            control.at[k, :, lanes(b, width)], held.at[b, pl.ds(0, rows)], held_sems.at[b]
        )

    def load_raw(c, act):
        @pl.when(c < chunks - 1)
        def _():
            act(pltpu.make_async_copy(
                ensemble.at[:, at_levels(c)], raw.at[:, at_levels(c)], raw_sems.at[c]))

        @pl.when(c == chunks - 1)
        def _():
            last = pl.ds(levels - tail, tail)
            act(pltpu.make_async_copy(
                ensemble.at[:, last], raw.at[:, last], raw_sems.at[c]))

    loop(0, chunks, lambda c: load_raw(c, lambda copy: copy.start()))
    loop(0, blocks, lambda b: load_control(0, b).start())
    load_inn = pltpu.make_async_copy(innovation, inn.at[pl.ds(0, rows)], fact_load_sems.at[0])
    load_inv = pltpu.make_async_copy(inverse, inv.at[pl.ds(0, rows)], fact_load_sems.at[1])
    load_inn.start()
    load_inv.start()

    barrier = pltpu.get_barrier_semaphore()
    loop(1, blocks, lambda t: pl.semaphore_signal(
        barrier, inc=1, device_id={"lon": lax.rem(me + t, blocks)}, device_id_type=MESH))
    when(has_below, lambda: pl.semaphore_signal(
        barrier, inc=1, device_id={"lat": row - 1}, device_id_type=MESH))
    when(has_above, lambda: pl.semaphore_signal(
        barrier, inc=1, device_id={"lat": row + 1}, device_id_type=MESH))
    inner = jnp.logical_and(has_below, has_above)
    when(inner, lambda: pl.semaphore_wait(barrier, blocks + 1))
    when(jnp.logical_not(inner), lambda: pl.semaphore_wait(barrier, blocks))

    def same_core(t):
        return lax.rem(chip + t, chips)

    def band_copy(slot, target):
        return remote(bands.at[slot], bands.at[slot], band_sems, (target,), (slot,), lon=target)

    def band_mate(slot, landed):
        return remote(bands.at[slot], bands.at[slot], band_mate_sems, (slot,), (landed,), lon=mate)

    def tap_copy(slot, target):
        return remote(all_taps.at[slot], all_taps.at[slot], tap_sems, (target,), (slot,), lon=target)

    bands[me] = band[...]
    all_taps[me] = taps[...]
    loop(1, chips, lambda t: band_copy(me, 2 * same_core(t) + core).start())
    band_mate(me, me).start()
    loop(1, blocks, lambda t: tap_copy(me, lax.rem(me + t, blocks)).start())

    def e_copy(c, target, slot):
        return remote(
            packed.at[target, :, :, at_levels(c)], own_e.at[slot, :, :, at_levels(c)],
            e_sems, (c, target), (c, slot), lon=target)

    def up_copy(c, s):
        return remote(
            own_e.at[s, :, pl.ds(height - half, half), at_levels(c)],
            below_e.at[s, :, :, at_levels(c)], up_sems, (c, s), (c, s), lat=row + 1)

    def down_copy(c, s):
        return remote(
            own_e.at[s, :, pl.ds(0, half), at_levels(c)],
            above_e.at[s, :, :, at_levels(c)], down_sems, (c, s), (c, s), lat=row - 1)

    def pass_on(c, s):
        when(has_above, lambda: up_copy(c, s).start())
        when(has_below, lambda: down_copy(c, s).start())

    def repack(place, target, c):
        for k in range(own):
            value = raw[place * own + k, at_levels(c)].astype(F32)
            turn[k] = value.reshape(GROUP * height, width)
            for y in range(height):
                target[k, y, at_levels(c), :] = turn[
                    k, pl.ds(y, GROUP, stride=height), :].astype(BF16)

    def clear_raw(m):
        for l in range(levels, padded):
            raw[m, l] = jnp.zeros((height, width), BF16)

    loop(0, members, clear_raw)

    def send_near(c):
        load_raw(c, lambda copy: copy.wait())
        repack(mate, packed.at[mate], c)
        e_copy(c, mate, me).start()
        repack(me, own_e.at[me], c)
        pass_on(c, me)

    def send_far(c):
        def other(t):
            p = lax.rem(2 * chip + t, blocks)
            repack(p, packed.at[p], c)
            e_copy(c, p, me).start()

        loop(2, blocks, other)

    def relay(c, s):
        e_copy(c, s, s).wait_recv()
        pass_on(c, s)

    def relay_far(c):
        loop(2, blocks, lambda t: relay(c, lax.rem(2 * chip + t, blocks)))

    loop(0, chunks, send_near)
    loop(0, chunks, send_far)
    loop(0, chunks, lambda c: relay(c, mate))

    edge = (blocks, own, half)
    zero_rows = jnp.zeros((padded, width), BF16)

    def clear_edges(target):
        def clear(b):
            for k in range(own):
                for y in range(half):
                    target[b, k, y] = zero_rows

        loop(0, blocks, clear)

    def clear_facts(first):
        def clear(j):
            for parity in range(2):
                for y in range(half):
                    facts[parity, j, first + y] = zero_rows

        loop(0, chips, clear)

    def clear_sums(target):
        def clear(j):
            for y in range(half):
                target[j, y] = zero_rows

        loop(0, chips, clear)

    def clear_below():
        clear_edges(below_e)
        clear_facts(0)
        clear_sums(below_sums)

    def clear_above():
        clear_edges(above_e)
        clear_facts(height + half)
        clear_sums(above_sums)

    when(jnp.logical_not(has_below), clear_below)
    when(jnp.logical_not(has_above), clear_above)
    inn[pl.ds(rows, padded * height - rows), :] = jnp.zeros((padded * height - rows, width), F32)
    inv[pl.ds(rows, padded * height - rows), :] = jnp.zeros((padded * height - rows, width), F32)

    def clear_tail(b):
        for k in range(own):
            for y in range(height):
                fields[k, y, pl.ds(padded - GROUP, GROUP), lanes(b, width)] = jnp.zeros(
                    (GROUP, width), BF16)

    loop(0, blocks, clear_tail)

    for k in range(own):
        if k > 0:
            relay_far(k - 1)

        def vertical(b):
            load_control(k, b).wait()
            columns = jnp.concatenate(
                [held[b, pl.ds(y, levels, stride=height), :] for y in range(height)], axis=1)
            out = jnp.dot(root[...], columns.astype(BF16), preferred_element_type=F32).astype(BF16)
            for y in range(height):
                fields[k, y, pl.ds(0, levels), lanes(b, width)] = out[:, y * width : (y + 1) * width]
            if k + 1 < own:
                load_control(k + 1, b).start()

        loop(0, blocks, vertical)
        if k == 0:
            def forward_band(t):
                s = 2 * same_core(t) + core
                band_copy(s, s).wait_recv()
                band_mate(s, s).start()

            loop(1, chips, forward_band)
            loop(0, chips, lambda j: band_mate(
                2 * j + 1 - core, 2 * j + 1 - core).wait_recv())
            loop(1, blocks, lambda t: tap_copy(
                lax.rem(me + t, blocks), lax.rem(me + t, blocks)).wait_recv())

        def longitude(b):
            parts = [
                fields[k, :, :, lanes(lax.rem(b + blocks + o, blocks), width)] for o in (-1, 0, 1)]
            left = jnp.concatenate([part.reshape(height * padded, width) for part in parts], axis=1)
            out = jnp.dot(left, bands[b], preferred_element_type=F32)
            spread[b, k] = out.astype(BF16).reshape(height, padded, width)

        loop(0, blocks, longitude)

    def tap_rows(s):
        return [
            jnp.broadcast_to(all_taps[s, pl.ds(o, 1), :], (GROUP, width))
            for o in range(2 * half + 1)]

    def e_row(s, k, r, c):
        if r < half:
            value = below_e[s, k, r, at_levels(c), :]
        elif r < half + height:
            value = own_e[s, k, r - half, at_levels(c), :]
        else:
            value = above_e[s, k, r - half - height, at_levels(c), :]
        return value.astype(F32)

    def stencil(s, c, put):
        tap = tap_rows(s)
        field = [
            [spread[s, k, y, at_levels(c), :].astype(F32) for y in range(height)]
            for k in range(own)]
        for r in range(extended):
            total = None
            for k in range(own):
                part = None
                for o in range(-half, half + 1):
                    y = r - half + o
                    if 0 <= y < height:
                        term = tap[o + half] * field[k][y]
                        part = term if part is None else part + term
                part = part * e_row(s, k, r, c)
                total = part if total is None else total + part
            put(r, total)

    def held_row(j, r, c):
        return 2 * j + r // height, pl.ds(
            pl.multiple_of((r % height) * padded + c * GROUP, GROUP), GROUP)

    def get_held(j, r, c):
        b, at = held_row(j, r, c)
        return held[b, at, :]

    def put_held(j, r, c, value):
        b, at = held_row(j, r, c)
        held[b, at, :] = value

    def core_copy(c, j):
        return remote(sums.at[j, :, at_levels(c)], mate_sums.at[j, :, at_levels(c)],
                      core_sems, (c, j), (c, j), lon=mate)

    def forward(c):
        def other(j):
            for parity in range(2):
                when(has_below, lambda: up_copy(c, 2 * j + parity).wait_recv())
                when(has_above, lambda: down_copy(c, 2 * j + parity).wait_recv())

            def put(r, value):
                sums[j, r, at_levels(c), :] = value.astype(BF16)

            stencil(2 * j + 1 - core, c, put)
            core_copy(c, j).start()

        loop(0, chips, other)
        loop(0, chips, lambda j: stencil(
            2 * j + core, c, lambda r, value: put_held(j, r, c, value)))

    def sum_up(c):
        return remote(sums.at[:, pl.ds(half + height, half), at_levels(c)],
                      below_sums.at[:, :, at_levels(c)], sum_sems, (c, 0), (c, 0), lat=row + 1)

    def sum_down(c):
        return remote(sums.at[:, pl.ds(0, half), at_levels(c)],
                      above_sums.at[:, :, at_levels(c)], sum_sems, (c, 1), (c, 1), lat=row - 1)

    def combine(c):
        def each(j):
            core_copy(c, j).wait()
            for r in range(extended):
                value = get_held(j, r, c) + mate_sums[j, r, at_levels(c), :].astype(F32)
                if half <= r < half + height:
                    put_held(j, r, c, value)
                else:
                    sums[j, r, at_levels(c), :] = value.astype(BF16)

        loop(0, chips, each)
        when(has_above, lambda: sum_up(c).start())
        when(has_below, lambda: sum_down(c).start())

    def lat_sum(j, y, c):
        value = get_held(j, half + y, c)
        if y < half:
            value = value + below_sums[j, y, at_levels(c), :].astype(F32)
        if y >= height - half:
            value = value + above_sums[j, y - height + half, at_levels(c), :].astype(F32)
        return value

    def chip_copy(c, target, slot):
        return remote(sums.at[target, pl.ds(half, height), at_levels(c)],
                      chip_sums.at[slot, :, at_levels(c)],
                      chip_sems, (c, target), (c, slot), lon=2 * target + core)

    def scatter(c):
        when(has_below, lambda: sum_up(c).wait_recv())
        when(has_above, lambda: sum_down(c).wait_recv())

        def each(t):
            j = same_core(t)
            for y in range(height):
                sums[j, half + y, at_levels(c), :] = lat_sum(j, y, c).astype(BF16)
            chip_copy(c, j, chip).start()

        loop(1, chips, each)

    def spread_copy(c, target, slot):
        own_rows = facts.at[core, slot, pl.ds(half, height), at_levels(c)]
        return remote(own_rows, own_rows, spread_sems, (c, target), (c, slot),
                      lon=2 * target + core)

    def depart(c):
        loop(1, chips, lambda t: chip_copy(c, same_core(t), same_core(t)).wait_recv())
        for y in range(height):
            value = lat_sum(chip, y, c)
            for t in range(1, chips):
                value = value + chip_sums[same_core(t), y, at_levels(c), :].astype(F32)
            at = pl.ds(c * GROUP * height + y, GROUP, stride=height)
            value = inv[at, :] * (value - inn[at, :])
            inn[at, :] = value
            facts[core, chip, half + y, at_levels(c), :] = value.astype(BF16)
        loop(1, chips, lambda t: spread_copy(c, same_core(t), chip).start())

    def fact_up(c):
        return remote(facts.at[core, :, pl.ds(height, half), at_levels(c)],
                      facts.at[core, :, pl.ds(0, half), at_levels(c)],
                      fact_sems, (c, 0), (c, 0), lat=row + 1)

    def fact_down(c):
        return remote(facts.at[core, :, pl.ds(half, half), at_levels(c)],
                      facts.at[core, :, pl.ds(half + height, half), at_levels(c)],
                      fact_sems, (c, 1), (c, 1), lat=row - 1)

    def mate_copy(c, part, parity):
        first, count = ((half, height), (0, half), (half + height, half))[part]
        piece = facts.at[parity, :, pl.ds(first, count), at_levels(c)]
        return remote(piece, piece, mate_sems, (c, part), (c, part), lon=mate)

    def gather(c):
        loop(1, chips, lambda t: spread_copy(c, same_core(t), same_core(t)).wait_recv())
        when(has_above, lambda: fact_up(c).start())
        when(has_below, lambda: fact_down(c).start())
        mate_copy(c, 0, core).start()

    def gather_edges(c):
        def below():
            fact_up(c).wait_recv()
            mate_copy(c, 1, core).start()

        def above():
            fact_down(c).wait_recv()
            mate_copy(c, 2, core).start()

        when(has_below, below)
        when(has_above, above)

    def out_copy(g):
        span = together * GROUP
        at = pl.ds(pl.multiple_of(g * span, span), span)
        return pltpu.make_async_copy(
            spread.at[:, :, :, at], summed.at[:, :, :, at], out_sems.at[g])

    def adjoint(c):
        mate_copy(c, 0, 1 - core).wait_recv()
        when(has_below, lambda: mate_copy(c, 1, 1 - core).wait_recv())
        when(has_above, lambda: mate_copy(c, 2, 1 - core).wait_recv())

        def each(s):
            tap = tap_rows(s)
            fact = [facts[lax.rem(s, 2), lax.div(s, 2), r, at_levels(c), :].astype(F32)
                    for r in range(extended)]
            for k in range(own):
                pulled = [e_row(s, k, r, c) * fact[r] for r in range(extended)]
                for y in range(height):
                    total = None
                    for o in range(-half, half + 1):
                        term = tap[o + half] * pulled[y - o + half]
                        total = term if total is None else total + term
                    fields[k, y, at_levels(c), lanes(s, width)] = total.astype(BF16)

        loop(0, blocks, each)

        if together == 1:
            adjoint_longitude(c)
        else:
            when(lax.rem(c, together) == together - 1,
                 lambda: adjoint_longitude(lax.div(c, together)))

    def adjoint_longitude(g):
        span = together * GROUP
        at = pl.ds(pl.multiple_of(g * span, span), span)

        def longitude(b):
            before, after = lax.rem(b + blocks - 1, blocks), lax.rem(b + 1, blocks)
            right = jnp.concatenate(
                [
                    bands[before, 2 * width : 3 * width],
                    bands[b, width : 2 * width],
                    bands[after, 0:width],
                ],
                axis=0,
            )
            left = jnp.concatenate(
                [
                    jnp.concatenate(
                        [fields[k, :, at, lanes(s, width)].reshape(height * span, width)
                         for k in range(own)], axis=0)
                    for s in (before, b, after)
                ],
                axis=1,
            )
            out = jnp.dot(left, right, preferred_element_type=F32).astype(BF16)
            spread[b, :, :, at, :] = out.reshape(own, height, span, width)

        loop(0, blocks, longitude)
        out_copy(g).start()

    def transpose_bands(b):
        for part in range(3):
            at = slice(part * width, (part + 1) * width)
            bands[b, at] = bands[b, at].astype(F32).T.astype(BF16)

    loop(1, chips, lambda t: band_copy(me, 2 * same_core(t) + core).wait_send())
    loop(0, chips, lambda j: band_mate(2 * j + core, 2 * j + core).wait_send())
    loop(0, blocks, transpose_bands)
    load_inn.wait()
    load_inv.wait()

    def stage(action, c):
        when(jnp.logical_and(c >= 0, c < chunks), lambda: action(c))

    def step(i):
        when(i < chunks, lambda: relay_far(i))
        stage(combine, i - OFFSETS[1])
        stage(scatter, i - OFFSETS[2])
        stage(depart, i - OFFSETS[3])
        stage(gather, i - OFFSETS[4])
        stage(gather_edges, i - OFFSETS[5])
        stage(forward, i - OFFSETS[0])
        stage(adjoint, i - OFFSETS[6])

    loop(own - 1, chunks + OFFSETS[6], step)
    store = pltpu.make_async_copy(inn.at[pl.ds(0, rows)], departure, dep_sem)
    store.start()

    def sent(c):
        loop(1, blocks, lambda t: e_copy(c, lax.rem(me + t, blocks), me).wait_send())
        loop(1, chips, lambda t: chip_copy(c, same_core(t), chip).wait_send())
        loop(1, chips, lambda t: spread_copy(c, same_core(t), chip).wait_send())
        mate_copy(c, 0, core).wait_send()

        def below():
            loop(0, blocks, lambda s: down_copy(c, s).wait_send())
            sum_down(c).wait_send()
            fact_down(c).wait_send()
            mate_copy(c, 1, core).wait_send()

        def above():
            loop(0, blocks, lambda s: up_copy(c, s).wait_send())
            sum_up(c).wait_send()
            fact_up(c).wait_send()
            mate_copy(c, 2, core).wait_send()

        when(has_below, below)
        when(has_above, above)

    loop(0, chunks // together, lambda g: out_copy(g).wait())
    loop(0, chunks, sent)
    loop(1, blocks, lambda t: tap_copy(me, lax.rem(me + t, blocks)).wait_send())
    store.wait()


def finish(control, summed, root, departure, gradient, result, held, part, facts, held_sems, part_sems, store_sems, sems):
    levels = root.shape[0]
    blocks, own, height, _, width = summed.shape
    taken = pltpu.make_async_copy(departure, facts, sems.at[0])
    given = pltpu.make_async_copy(facts, result, sems.at[1])

    def place(i):
        return lax.div(i, blocks), lax.rem(i, blocks)

    def load_control(i):
        k, b = place(i)
        return pltpu.make_async_copy(control.at[k, :, lanes(b, width)], held.at[i], held_sems.at[i])

    def load_part(i):
        k, b = place(i)
        return pltpu.make_async_copy(summed.at[b, k], part.at[i], part_sems.at[i])

    def store(i):
        k, b = place(i)
        return pltpu.make_async_copy(held.at[i], gradient.at[k, :, lanes(b, width)], store_sems.at[i])

    def start(i):
        load_part(i).start()
        load_control(i).start()

    def work(i):
        load_part(i).wait()
        right = jnp.concatenate([part[i, y, 0:levels, :] for y in range(height)], axis=1)
        out = lax.dot_general(
            root[...], right, (((0,), (0,)), ((), ())), preferred_element_type=F32)
        out = out.astype(BF16).astype(F32)
        load_control(i).wait()
        for y in range(height):
            at = pl.ds(y, levels, stride=height)
            held[i, at, :] = held[i, at, :] + out[:, y * width : (y + 1) * width]
        store(i).start()

    taken.start()
    loop(0, own * blocks, start)
    taken.wait()
    given.start()
    loop(0, own * blocks, work)
    loop(0, own * blocks, lambda i: store(i).wait())
    given.wait()


def shards(control, ensemble, vertical_root, sector_band, latitude_taps, innovation, inverse_error):
    spans = latitude_taps.shape[0]
    half = spans // 2
    width = sector_band.shape[1]
    own, levels, height, total = control.shape
    members = ensemble.shape[0]
    blocks = total // width
    chips = blocks // 2
    chunks = -(-levels // GROUP)
    padded = chunks * GROUP
    rows = levels * height
    extended = height + 2 * half
    fields = control.reshape(own, rows, total)
    band = sector_band.reshape(3 * width, width)
    dma = pltpu.SemaphoreType.DMA
    vmem = pltpu.VMEM
    local = pl.BlockSpec(memory_space=pltpu.VMEM)
    anywhere = pl.BlockSpec(memory_space=pl.ANY)
    whole = (blocks, own, height, padded, width)
    edges = (blocks, own, half, padded, width)
    summed, departure = pl.pallas_call(
        program,
        in_specs=[anywhere, anywhere, local, local, local, anywhere, anywhere],
        out_specs=[anywhere, anywhere],
        out_shape=[
            jax.ShapeDtypeStruct(whole, BF16),
            jax.ShapeDtypeStruct((rows, width), F32),
        ],
        scratch_shapes=[
            vmem((blocks, height * padded, width), F32),
            vmem((members, padded, height, width), BF16),
            vmem((own, GROUP * height, width), F32),
            vmem(whole, BF16),
            vmem(whole, BF16),
            vmem(edges, BF16),
            vmem(edges, BF16),
            vmem(whole, BF16),
            vmem((own, height, padded, total), BF16),
            vmem((chips, extended, padded, width), BF16),
            vmem((chips, extended, padded, width), BF16),
            vmem((chips, half, padded, width), BF16),
            vmem((chips, half, padded, width), BF16),
            vmem((chips, height, padded, width), BF16),
            vmem((2, chips, extended, padded, width), BF16),
            vmem((padded * height, width), F32),
            vmem((padded * height, width), F32),
            vmem((blocks, 3 * width, width), BF16),
            vmem((blocks, spans, width), F32),
            dma((blocks,)),
            dma((chunks,)),
            dma((2,)),
            dma((chunks,)),
            dma,
            dma((2, chunks, blocks)),
            dma((2, chunks, blocks)),
            dma((2, chunks, blocks)),
            dma((2, chunks, chips)),
            dma((2, chunks, 2)),
            dma((2, chunks, chips)),
            dma((2, chunks, chips)),
            dma((2, chunks, 2)),
            dma((2, chunks, 3)),
            dma((2, blocks)),
            dma((2, blocks)),
            dma((2, blocks)),
        ],
        compiler_params=pltpu.CompilerParams(
            vmem_limit_bytes=VMEM_LIMIT, collective_id=0, has_side_effects=True
        ),
        name="exchange",
    )(fields, ensemble, vertical_root, band, latitude_taps,
      innovation.reshape(rows, width), inverse_error.reshape(rows, width))
    gradient, departure = pl.pallas_call(
        finish,
        in_specs=[anywhere, anywhere, local, anywhere],
        out_specs=[anywhere, anywhere],
        out_shape=[
            jax.ShapeDtypeStruct((own, rows, total), F32),
            jax.ShapeDtypeStruct((rows, width), F32),
        ],
        scratch_shapes=[
            vmem((own * blocks, rows, width), F32),
            vmem((own * blocks, height, padded, width), BF16),
            vmem((rows, width), F32),
            dma((own * blocks,)),
            dma((own * blocks,)),
            dma((own * blocks,)),
            dma((2,)),
        ],
        compiler_params=pltpu.CompilerParams(vmem_limit_bytes=VMEM_LIMIT),
        name="finish",
    )(fields, summed, vertical_root, departure)
    return gradient.reshape(control.shape), departure.reshape(innovation.shape)


def solution(mesh):
    placed = (
        P("lon", None, "lat", None),
        P(None, None, "lat", "lon"),
        P(),
        P(None, None, "lon"),
        P(None, "lon"),
        P(None, "lat", "lon"),
        P(None, "lat", "lon"),
    )
    return jax.shard_map(
        shards,
        mesh=mesh,
        in_specs=placed,
        out_specs=(P("lon", None, "lat", None), P(None, "lat", "lon")),
        check_vma=False,
    )
```

```python
import functools

import jax
import jax.numpy as jnp
from jax import lax
from jax.experimental import pallas as pl
from jax.experimental.pallas import tpu as pltpu
from jax.sharding import PartitionSpec as P

F32, BF16 = jnp.float32, jnp.bfloat16
VMEM_LIMIT = 62 * 1024 * 1024
GROUP = 16
OFFSETS = (1, 3, 4, 7, 9, 10, 12)
MESH = pl.DeviceIdType.MESH


def lanes(block, width):
    return pl.ds(pl.multiple_of(block * width, width), width)


def loop(start, stop, body, unroll=1):
    def step(i, _):
        body(i)
        return 0

    lax.fori_loop(start, stop, step, 0, unroll=unroll)


def program(
    control, ensemble, root, band, taps, innovation, inverse,
    summed, departure,
    held, raw, turn, packed, own_e, below_e, above_e, spread, fields,
    sums, mate_sums, below_sums, above_sums, chip_sums, facts,
    inn, inv, bands, all_taps,
    held_sems, raw_sems, fact_load_sems, out_sems, dep_sem,
    e_sems, up_sems, down_sems, core_sems, sum_sems, chip_sems, spread_sems,
    fact_sems, mate_sems, band_sems, band_mate_sems, tap_sems,
):
    blocks, own, height, padded, width = packed.shape
    levels, members = root.shape[0], blocks * own
    rows = levels * height
    half = taps.shape[0] // 2
    extended = height + 2 * half
    chips = blocks // 2
    chunks = padded // GROUP
    together = 3 if chunks % 3 == 0 else 1
    tail = levels - (chunks - 1) * GROUP
    me, row = lax.axis_index("lon"), lax.axis_index("lat")
    core = lax.rem(me, 2)
    chip = lax.div(me, 2)
    mate = me + 1 - 2 * core
    has_below, has_above = row > 0, row < lax.axis_size("lat") - 1

    def at_levels(c):
        return pl.ds(pl.multiple_of(c * GROUP, GROUP), GROUP)

    def remote(source, target, sems, sent, landed, **device):
        return pltpu.make_async_remote_copy(
            src_ref=source, dst_ref=target, send_sem=sems.at[(0,) + sent],
            recv_sem=sems.at[(1,) + landed], device_id=device, device_id_type=MESH,
        )

    def when(guard, action):
        @pl.when(guard)
        def _():
            action()

    def load_control(k, b):
        return pltpu.make_async_copy(
            control.at[k, :, lanes(b, width)], held.at[b, pl.ds(0, rows)], held_sems.at[b]
        )

    def load_raw(c, act):
        @pl.when(c < chunks - 1)
        def _():
            act(pltpu.make_async_copy(
                ensemble.at[:, at_levels(c)], raw.at[:, at_levels(c)], raw_sems.at[c]))

        @pl.when(c == chunks - 1)
        def _():
            last = pl.ds(levels - tail, tail)
            act(pltpu.make_async_copy(
                ensemble.at[:, last], raw.at[:, last], raw_sems.at[c]))

    loop(0, chunks, lambda c: load_raw(c, lambda copy: copy.start()))
    loop(0, blocks, lambda b: load_control(0, b).start())
    load_inn = pltpu.make_async_copy(innovation, inn.at[pl.ds(0, rows)], fact_load_sems.at[0])
    load_inv = pltpu.make_async_copy(inverse, inv.at[pl.ds(0, rows)], fact_load_sems.at[1])
    load_inn.start()
    load_inv.start()

    barrier = pltpu.get_barrier_semaphore()
    loop(1, blocks, lambda t: pl.semaphore_signal(
        barrier, inc=1, device_id={"lon": lax.rem(me + t, blocks)}, device_id_type=MESH))
    when(has_below, lambda: pl.semaphore_signal(
        barrier, inc=1, device_id={"lat": row - 1}, device_id_type=MESH))
    when(has_above, lambda: pl.semaphore_signal(
        barrier, inc=1, device_id={"lat": row + 1}, device_id_type=MESH))
    inner = jnp.logical_and(has_below, has_above)
    when(inner, lambda: pl.semaphore_wait(barrier, blocks + 1))
    when(jnp.logical_not(inner), lambda: pl.semaphore_wait(barrier, blocks))

    def same_core(t):
        return lax.rem(chip + t, chips)

    def band_copy(slot, target):
        return remote(bands.at[slot], bands.at[slot], band_sems, (target,), (slot,), lon=target)

    def band_mate(slot, landed):
        return remote(bands.at[slot], bands.at[slot], band_mate_sems, (slot,), (landed,), lon=mate)

    def tap_copy(slot, target):
        return remote(all_taps.at[slot], all_taps.at[slot], tap_sems, (target,), (slot,), lon=target)

    bands[me] = band[...]
    all_taps[me] = taps[...]
    loop(1, chips, lambda t: band_copy(me, 2 * same_core(t) + core).start())
    band_mate(me, me).start()
    loop(1, blocks, lambda t: tap_copy(me, lax.rem(me + t, blocks)).start())

    def e_copy(c, target, slot):
        return remote(
            packed.at[target, :, :, at_levels(c)], own_e.at[slot, :, :, at_levels(c)],
            e_sems, (c, target), (c, slot), lon=target)

    def up_copy(c, s):
        return remote(
            own_e.at[s, :, pl.ds(height - half, half), at_levels(c)],
            below_e.at[s, :, :, at_levels(c)], up_sems, (c, s), (c, s), lat=row + 1)

    def down_copy(c, s):
        return remote(
            own_e.at[s, :, pl.ds(0, half), at_levels(c)],
            above_e.at[s, :, :, at_levels(c)], down_sems, (c, s), (c, s), lat=row - 1)

    def pass_on(c, s):
        when(has_above, lambda: up_copy(c, s).start())
        when(has_below, lambda: down_copy(c, s).start())

    def repack(place, target, c):
        for k in range(own):
            value = raw[place * own + k, at_levels(c)].astype(F32)
            turn[k] = value.reshape(GROUP * height, width)
            for y in range(height):
                target[k, y, at_levels(c), :] = turn[
                    k, pl.ds(y, GROUP, stride=height), :].astype(BF16)

    def clear_raw(m):
        for l in range(levels, padded):
            raw[m, l] = jnp.zeros((height, width), BF16)

    loop(0, members, clear_raw)

    def send_near(c):
        load_raw(c, lambda copy: copy.wait())
        repack(mate, packed.at[mate], c)
        e_copy(c, mate, me).start()
        repack(me, own_e.at[me], c)
        pass_on(c, me)

    def send_far(c):
        def other(t):
            p = lax.rem(2 * chip + t, blocks)
            repack(p, packed.at[p], c)
            e_copy(c, p, me).start()

        loop(2, blocks, other)

    def relay(c, s):
        e_copy(c, s, s).wait_recv()
        pass_on(c, s)

    def relay_far(c):
        loop(2, blocks, lambda t: relay(c, lax.rem(2 * chip + t, blocks)))

    loop(0, chunks, send_near)
    loop(0, chunks, send_far)
    loop(0, chunks, lambda c: relay(c, mate))

    edge = (blocks, own, half)
    zero_rows = jnp.zeros((padded, width), BF16)

    def clear_edges(target):
        def clear(b):
            for k in range(own):
                for y in range(half):
                    target[b, k, y] = zero_rows

        loop(0, blocks, clear)

    def clear_facts(first):
        def clear(j):
            for parity in range(2):
                for y in range(half):
                    facts[parity, j, first + y] = zero_rows

        loop(0, chips, clear)

    def clear_sums(target):
        def clear(j):
            for y in range(half):
                target[j, y] = zero_rows

        loop(0, chips, clear)

    def clear_below():
        clear_edges(below_e)
        clear_facts(0)
        clear_sums(below_sums)

    def clear_above():
        clear_edges(above_e)
        clear_facts(height + half)
        clear_sums(above_sums)

    when(jnp.logical_not(has_below), clear_below)
    when(jnp.logical_not(has_above), clear_above)
    inn[pl.ds(rows, padded * height - rows), :] = jnp.zeros((padded * height - rows, width), F32)
    inv[pl.ds(rows, padded * height - rows), :] = jnp.zeros((padded * height - rows, width), F32)

    def clear_tail(b):
        for k in range(own):
            for y in range(height):
                fields[k, y, pl.ds(padded - GROUP, GROUP), lanes(b, width)] = jnp.zeros(
                    (GROUP, width), BF16)

    loop(0, blocks, clear_tail)

    for k in range(own):
        if k > 0:
            relay_far(k - 1)

        def vertical(b):
            load_control(k, b).wait()
            columns = jnp.concatenate(
                [held[b, pl.ds(y, levels, stride=height), :] for y in range(height)], axis=1)
            out = jnp.dot(root[...], columns.astype(BF16), preferred_element_type=F32).astype(BF16)
            for y in range(height):
                fields[k, y, pl.ds(0, levels), lanes(b, width)] = out[:, y * width : (y + 1) * width]
            if k + 1 < own:
                load_control(k + 1, b).start()

        loop(0, blocks, vertical)
        if k == 0:
            def forward_band(t):
                s = 2 * same_core(t) + core
                band_copy(s, s).wait_recv()
                band_mate(s, s).start()

            loop(1, chips, forward_band)
            loop(0, chips, lambda j: band_mate(
                2 * j + 1 - core, 2 * j + 1 - core).wait_recv())
            loop(1, blocks, lambda t: tap_copy(
                lax.rem(me + t, blocks), lax.rem(me + t, blocks)).wait_recv())

        def longitude(b):
            parts = [
                fields[k, :, :, lanes(lax.rem(b + blocks + o, blocks), width)] for o in (-1, 0, 1)]
            left = jnp.concatenate([part.reshape(height * padded, width) for part in parts], axis=1)
            out = jnp.dot(left, bands[b], preferred_element_type=F32)
            spread[b, k] = out.astype(BF16).reshape(height, padded, width)

        loop(0, blocks, longitude)

    def tap_rows(s):
        return [
            jnp.broadcast_to(all_taps[s, pl.ds(o, 1), :], (GROUP, width))
            for o in range(2 * half + 1)]

    def e_row(s, k, r, c):
        if r < half:
            value = below_e[s, k, r, at_levels(c), :]
        elif r < half + height:
            value = own_e[s, k, r - half, at_levels(c), :]
        else:
            value = above_e[s, k, r - half - height, at_levels(c), :]
        return value.astype(F32)

    def stencil(s, c, put):
        tap = tap_rows(s)
        field = [
            [spread[s, k, y, at_levels(c), :].astype(F32) for y in range(height)]
            for k in range(own)]
        for r in range(extended):
            total = None
            for k in range(own):
                part = None
                for o in range(-half, half + 1):
                    y = r - half + o
                    if 0 <= y < height:
                        term = tap[o + half] * field[k][y]
                        part = term if part is None else part + term
                part = part * e_row(s, k, r, c)
                total = part if total is None else total + part
            put(r, total)

    def held_row(j, r, c):
        return 2 * j + r // height, pl.ds(
            pl.multiple_of((r % height) * padded + c * GROUP, GROUP), GROUP)

    def get_held(j, r, c):
        b, at = held_row(j, r, c)
        return held[b, at, :]

    def put_held(j, r, c, value):
        b, at = held_row(j, r, c)
        held[b, at, :] = value

    def core_copy(c, j):
        return remote(sums.at[j, :, at_levels(c)], mate_sums.at[j, :, at_levels(c)],
                      core_sems, (c, j), (c, j), lon=mate)

    def forward(c):
        def other(j):
            for parity in range(2):
                when(has_below, lambda: up_copy(c, 2 * j + parity).wait_recv())
                when(has_above, lambda: down_copy(c, 2 * j + parity).wait_recv())

            def put(r, value):
                sums[j, r, at_levels(c), :] = value.astype(BF16)

            stencil(2 * j + 1 - core, c, put)
            core_copy(c, j).start()

        loop(0, chips, other)
        loop(0, chips, lambda j: stencil(
            2 * j + core, c, lambda r, value: put_held(j, r, c, value)))

    def sum_up(c):
        return remote(sums.at[:, pl.ds(half + height, half), at_levels(c)],
                      below_sums.at[:, :, at_levels(c)], sum_sems, (c, 0), (c, 0), lat=row + 1)

    def sum_down(c):
        return remote(sums.at[:, pl.ds(0, half), at_levels(c)],
                      above_sums.at[:, :, at_levels(c)], sum_sems, (c, 1), (c, 1), lat=row - 1)

    def combine(c):
        def each(j):
            core_copy(c, j).wait()
            for r in range(extended):
                value = get_held(j, r, c) + mate_sums[j, r, at_levels(c), :].astype(F32)
                if half <= r < half + height:
                    put_held(j, r, c, value)
                else:
                    sums[j, r, at_levels(c), :] = value.astype(BF16)

        loop(0, chips, each)
        when(has_above, lambda: sum_up(c).start())
        when(has_below, lambda: sum_down(c).start())

    def lat_sum(j, y, c):
        value = get_held(j, half + y, c)
        if y < half:
            value = value + below_sums[j, y, at_levels(c), :].astype(F32)
        if y >= height - half:
            value = value + above_sums[j, y - height + half, at_levels(c), :].astype(F32)
        return value

    def chip_copy(c, target, slot):
        return remote(sums.at[target, pl.ds(half, height), at_levels(c)],
                      chip_sums.at[slot, :, at_levels(c)],
                      chip_sems, (c, target), (c, slot), lon=2 * target + core)

    def scatter(c):
        when(has_below, lambda: sum_up(c).wait_recv())
        when(has_above, lambda: sum_down(c).wait_recv())

        def each(t):
            j = same_core(t)
            for y in range(height):
                sums[j, half + y, at_levels(c), :] = lat_sum(j, y, c).astype(BF16)
            chip_copy(c, j, chip).start()

        loop(1, chips, each)

    def spread_copy(c, target, slot):
        own_rows = facts.at[core, slot, pl.ds(half, height), at_levels(c)]
        return remote(own_rows, own_rows, spread_sems, (c, target), (c, slot),
                      lon=2 * target + core)

    def depart(c):
        loop(1, chips, lambda t: chip_copy(c, same_core(t), same_core(t)).wait_recv())
        for y in range(height):
            value = lat_sum(chip, y, c)
            for t in range(1, chips):
                value = value + chip_sums[same_core(t), y, at_levels(c), :].astype(F32)
            at = pl.ds(c * GROUP * height + y, GROUP, stride=height)
            value = inv[at, :] * (value - inn[at, :])
            inn[at, :] = value
            facts[core, chip, half + y, at_levels(c), :] = value.astype(BF16)
        loop(1, chips, lambda t: spread_copy(c, same_core(t), chip).start())

    def fact_up(c):
        return remote(facts.at[core, :, pl.ds(height, half), at_levels(c)],
                      facts.at[core, :, pl.ds(0, half), at_levels(c)],
                      fact_sems, (c, 0), (c, 0), lat=row + 1)

    def fact_down(c):
        return remote(facts.at[core, :, pl.ds(half, half), at_levels(c)],
                      facts.at[core, :, pl.ds(half + height, half), at_levels(c)],
                      fact_sems, (c, 1), (c, 1), lat=row - 1)

    def mate_copy(c, part, parity):
        first, count = ((half, height), (0, half), (half + height, half))[part]
        piece = facts.at[parity, :, pl.ds(first, count), at_levels(c)]
        return remote(piece, piece, mate_sems, (c, part), (c, part), lon=mate)

    def gather(c):
        loop(1, chips, lambda t: spread_copy(c, same_core(t), same_core(t)).wait_recv())
        when(has_above, lambda: fact_up(c).start())
        when(has_below, lambda: fact_down(c).start())
        mate_copy(c, 0, core).start()

    def gather_edges(c):
        def below():
            fact_up(c).wait_recv()
            mate_copy(c, 1, core).start()

        def above():
            fact_down(c).wait_recv()
            mate_copy(c, 2, core).start()

        when(has_below, below)
        when(has_above, above)

    def out_copy(g):
        span = together * GROUP
        at = pl.ds(pl.multiple_of(g * span, span), span)
        return pltpu.make_async_copy(
            spread.at[:, :, :, at], summed.at[:, :, :, at], out_sems.at[g])

    def adjoint(c):
        mate_copy(c, 0, 1 - core).wait_recv()
        when(has_below, lambda: mate_copy(c, 1, 1 - core).wait_recv())
        when(has_above, lambda: mate_copy(c, 2, 1 - core).wait_recv())

        def each(s):
            tap = tap_rows(s)
            fact = [facts[lax.rem(s, 2), lax.div(s, 2), r, at_levels(c), :].astype(F32)
                    for r in range(extended)]
            for k in range(own):
                pulled = [e_row(s, k, r, c) * fact[r] for r in range(extended)]
                for y in range(height):
                    total = None
                    for o in range(-half, half + 1):
                        term = tap[o + half] * pulled[y - o + half]
                        total = term if total is None else total + term
                    fields[k, y, at_levels(c), lanes(s, width)] = total.astype(BF16)

        loop(0, blocks, each)

        if together == 1:
            adjoint_longitude(c)
        else:
            when(lax.rem(c, together) == together - 1,
                 lambda: adjoint_longitude(lax.div(c, together)))

    def adjoint_longitude(g):
        span = together * GROUP
        at = pl.ds(pl.multiple_of(g * span, span), span)

        def longitude(b):
            before, after = lax.rem(b + blocks - 1, blocks), lax.rem(b + 1, blocks)
            right = jnp.concatenate(
                [
                    bands[before, 2 * width : 3 * width],
                    bands[b, width : 2 * width],
                    bands[after, 0:width],
                ],
                axis=0,
            )
            left = jnp.concatenate(
                [
                    jnp.concatenate(
                        [fields[k, :, at, lanes(s, width)].reshape(height * span, width)
                         for k in range(own)], axis=0)
                    for s in (before, b, after)
                ],
                axis=1,
            )
            out = jnp.dot(left, right, preferred_element_type=F32).astype(BF16)
            spread[b, :, :, at, :] = out.reshape(own, height, span, width)

        loop(0, blocks, longitude)
        out_copy(g).start()

    def transpose_bands(b):
        for part in range(3):
            at = slice(part * width, (part + 1) * width)
            bands[b, at] = bands[b, at].astype(F32).T.astype(BF16)

    loop(1, chips, lambda t: band_copy(me, 2 * same_core(t) + core).wait_send())
    loop(0, chips, lambda j: band_mate(2 * j + core, 2 * j + core).wait_send())
    loop(0, blocks, transpose_bands)
    load_inn.wait()
    load_inv.wait()

    def stage(action, c):
        when(jnp.logical_and(c >= 0, c < chunks), lambda: action(c))

    def step(i):
        when(i < chunks, lambda: relay_far(i))
        stage(combine, i - OFFSETS[1])
        stage(scatter, i - OFFSETS[2])
        stage(depart, i - OFFSETS[3])
        stage(gather, i - OFFSETS[4])
        stage(gather_edges, i - OFFSETS[5])
        stage(forward, i - OFFSETS[0])
        stage(adjoint, i - OFFSETS[6])

    loop(own - 1, chunks + OFFSETS[6], step)
    store = pltpu.make_async_copy(inn.at[pl.ds(0, rows)], departure, dep_sem)
    store.start()

    def sent(c):
        loop(1, blocks, lambda t: e_copy(c, lax.rem(me + t, blocks), me).wait_send())
        loop(1, chips, lambda t: chip_copy(c, same_core(t), chip).wait_send())
        loop(1, chips, lambda t: spread_copy(c, same_core(t), chip).wait_send())
        mate_copy(c, 0, core).wait_send()

        def below():
            loop(0, blocks, lambda s: down_copy(c, s).wait_send())
            sum_down(c).wait_send()
            fact_down(c).wait_send()
            mate_copy(c, 1, core).wait_send()

        def above():
            loop(0, blocks, lambda s: up_copy(c, s).wait_send())
            sum_up(c).wait_send()
            fact_up(c).wait_send()
            mate_copy(c, 2, core).wait_send()

        when(has_below, below)
        when(has_above, above)

    loop(0, chunks // together, lambda g: out_copy(g).wait())
    loop(0, chunks, sent)
    loop(1, blocks, lambda t: tap_copy(me, lax.rem(me + t, blocks)).wait_send())
    store.wait()


def finish(control, summed, root, departure, gradient, result, held, part, facts, held_sems, part_sems, store_sems, sems):
    levels = root.shape[0]
    blocks, own, height, _, width = summed.shape
    taken = pltpu.make_async_copy(departure, facts, sems.at[0])
    given = pltpu.make_async_copy(facts, result, sems.at[1])

    def place(i):
        return lax.div(i, blocks), lax.rem(i, blocks)

    def load_control(i):
        k, b = place(i)
        return pltpu.make_async_copy(control.at[k, :, lanes(b, width)], held.at[i], held_sems.at[i])

    def load_part(i):
        k, b = place(i)
        return pltpu.make_async_copy(summed.at[b, k], part.at[i], part_sems.at[i])

    def store(i):
        k, b = place(i)
        return pltpu.make_async_copy(held.at[i], gradient.at[k, :, lanes(b, width)], store_sems.at[i])

    def start(i):
        load_part(i).start()
        load_control(i).start()

    def work(i):
        load_part(i).wait()
        right = jnp.concatenate([part[i, y, 0:levels, :] for y in range(height)], axis=1)
        out = lax.dot_general(
            root[...], right, (((0,), (0,)), ((), ())), preferred_element_type=F32)
        out = out.astype(BF16).astype(F32)
        load_control(i).wait()
        for y in range(height):
            at = pl.ds(y, levels, stride=height)
            held[i, at, :] = held[i, at, :] + out[:, y * width : (y + 1) * width]
        store(i).start()

    taken.start()
    loop(0, own * blocks, start)
    taken.wait()
    given.start()
    loop(0, own * blocks, work)
    loop(0, own * blocks, lambda i: store(i).wait())
    given.wait()


def shards(control, ensemble, vertical_root, sector_band, latitude_taps, innovation, inverse_error):
    spans = latitude_taps.shape[0]
    half = spans // 2
    width = sector_band.shape[1]
    own, levels, height, total = control.shape
    members = ensemble.shape[0]
    blocks = total // width
    chips = blocks // 2
    chunks = -(-levels // GROUP)
    padded = chunks * GROUP
    rows = levels * height
    extended = height + 2 * half
    fields = control.reshape(own, rows, total)
    band = sector_band.reshape(3 * width, width)
    dma = pltpu.SemaphoreType.DMA
    vmem = pltpu.VMEM
    local = pl.BlockSpec(memory_space=pltpu.VMEM)
    anywhere = pl.BlockSpec(memory_space=pl.ANY)
    whole = (blocks, own, height, padded, width)
    edges = (blocks, own, half, padded, width)
    summed, departure = pl.pallas_call(
        program,
        in_specs=[anywhere, anywhere, local, local, local, anywhere, anywhere],
        out_specs=[anywhere, anywhere],
        out_shape=[
            jax.ShapeDtypeStruct(whole, BF16),
            jax.ShapeDtypeStruct((rows, width), F32),
        ],
        scratch_shapes=[
            vmem((blocks, height * padded, width), F32),
            vmem((members, padded, height, width), BF16),
            vmem((own, GROUP * height, width), F32),
            vmem(whole, BF16),
            vmem(whole, BF16),
            vmem(edges, BF16),
            vmem(edges, BF16),
            vmem(whole, BF16),
            vmem((own, height, padded, total), BF16),
            vmem((chips, extended, padded, width), BF16),
            vmem((chips, extended, padded, width), BF16),
            vmem((chips, half, padded, width), BF16),
            vmem((chips, half, padded, width), BF16),
            vmem((chips, height, padded, width), BF16),
            vmem((2, chips, extended, padded, width), BF16),
            vmem((padded * height, width), F32),
            vmem((padded * height, width), F32),
            vmem((blocks, 3 * width, width), BF16),
            vmem((blocks, spans, width), F32),
            dma((blocks,)),
            dma((chunks,)),
            dma((2,)),
            dma((chunks,)),
            dma,
            dma((2, chunks, blocks)),
            dma((2, chunks, blocks)),
            dma((2, chunks, blocks)),
            dma((2, chunks, chips)),
            dma((2, chunks, 2)),
            dma((2, chunks, chips)),
            dma((2, chunks, chips)),
            dma((2, chunks, 2)),
            dma((2, chunks, 3)),
            dma((2, blocks)),
            dma((2, blocks)),
            dma((2, blocks)),
        ],
        compiler_params=pltpu.CompilerParams(
            vmem_limit_bytes=VMEM_LIMIT, collective_id=0, has_side_effects=True
        ),
        name="exchange",
    )(fields, ensemble, vertical_root, band, latitude_taps,
      innovation.reshape(rows, width), inverse_error.reshape(rows, width))
    gradient, departure = pl.pallas_call(
        finish,
        in_specs=[anywhere, anywhere, local, anywhere],
        out_specs=[anywhere, anywhere],
        out_shape=[
            jax.ShapeDtypeStruct((own, rows, total), F32),
            jax.ShapeDtypeStruct((rows, width), F32),
        ],
        scratch_shapes=[
            vmem((own * blocks, rows, width), F32),
            vmem((own * blocks, height, padded, width), BF16),
            vmem((rows, width), F32),
            dma((own * blocks,)),
            dma((own * blocks,)),
            dma((own * blocks,)),
            dma((2,)),
        ],
        compiler_params=pltpu.CompilerParams(vmem_limit_bytes=VMEM_LIMIT),
        name="finish",
    )(fields, summed, vertical_root, departure)
    return gradient.reshape(control.shape), departure.reshape(innovation.shape)


def solution(mesh):
    placed = (
        P("lon", None, "lat", None),
        P(None, None, "lat", "lon"),
        P(),
        P(None, None, "lon"),
        P(None, "lon"),
        P(None, "lat", "lon"),
        P(None, "lat", "lon"),
    )
    return jax.shard_map(
        shards,
        mesh=mesh,
        in_specs=placed,
        out_specs=(P("lon", None, "lat", None), P(None, "lat", "lon")),
        check_vma=False,
    )
```

```python
import functools

import jax
import jax.numpy as jnp
from jax import lax
from jax.experimental import pallas as pl
from jax.experimental.pallas import tpu as pltpu
from jax.sharding import PartitionSpec as P

F32, BF16 = jnp.float32, jnp.bfloat16
VMEM_LIMIT = 62 * 1024 * 1024
GROUP = 16
OFFSETS = (1, 3, 4, 7, 9, 11, 12)
MESH = pl.DeviceIdType.MESH


def lanes(block, width):
    return pl.ds(pl.multiple_of(block * width, width), width)


def loop(start, stop, body, unroll=1):
    def step(i, _):
        body(i)
        return 0

    lax.fori_loop(start, stop, step, 0, unroll=unroll)


def program(
    control, ensemble, root, band, taps, innovation, inverse,
    summed, departure,
    held, raw, turn, packed, own_e, below_e, above_e, spread, fields,
    sums, mate_sums, below_sums, above_sums, chip_sums, facts,
    inn, inv, bands, all_taps,
    held_sems, raw_sems, fact_load_sems, out_sems, dep_sem,
    e_sems, up_sems, down_sems, core_sems, sum_sems, chip_sems, spread_sems,
    fact_sems, mate_sems, band_sems, band_mate_sems, tap_sems,
):
    blocks, own, height, padded, width = packed.shape
    levels, members = root.shape[0], blocks * own
    rows = levels * height
    half = taps.shape[0] // 2
    extended = height + 2 * half
    chips = blocks // 2
    chunks = padded // GROUP
    together = 3 if chunks % 3 == 0 else 1
    tail = levels - (chunks - 1) * GROUP
    me, row = lax.axis_index("lon"), lax.axis_index("lat")
    core = lax.rem(me, 2)
    chip = lax.div(me, 2)
    mate = me + 1 - 2 * core
    has_below, has_above = row > 0, row < lax.axis_size("lat") - 1

    def at_levels(c):
        return pl.ds(pl.multiple_of(c * GROUP, GROUP), GROUP)

    def remote(source, target, sems, sent, landed, **device):
        return pltpu.make_async_remote_copy(
            src_ref=source, dst_ref=target, send_sem=sems.at[(0,) + sent],
            recv_sem=sems.at[(1,) + landed], device_id=device, device_id_type=MESH,
        )

    def when(guard, action):
        @pl.when(guard)
        def _():
            action()

    def load_control(k, b):
        return pltpu.make_async_copy(
            control.at[k, :, lanes(b, width)], held.at[b, pl.ds(0, rows)], held_sems.at[b]
        )

    def load_raw(c, act):
        @pl.when(c < chunks - 1)
        def _():
            act(pltpu.make_async_copy(
                ensemble.at[:, at_levels(c)], raw.at[:, at_levels(c)], raw_sems.at[c]))

        @pl.when(c == chunks - 1)
        def _():
            last = pl.ds(levels - tail, tail)
            act(pltpu.make_async_copy(
                ensemble.at[:, last], raw.at[:, last], raw_sems.at[c]))

    loop(0, chunks, lambda c: load_raw(c, lambda copy: copy.start()))
    loop(0, blocks, lambda b: load_control(0, b).start())
    load_inn = pltpu.make_async_copy(innovation, inn.at[pl.ds(0, rows)], fact_load_sems.at[0])
    load_inv = pltpu.make_async_copy(inverse, inv.at[pl.ds(0, rows)], fact_load_sems.at[1])
    load_inn.start()
    load_inv.start()

    barrier = pltpu.get_barrier_semaphore()
    loop(1, blocks, lambda t: pl.semaphore_signal(
        barrier, inc=1, device_id={"lon": lax.rem(me + t, blocks)}, device_id_type=MESH))
    when(has_below, lambda: pl.semaphore_signal(
        barrier, inc=1, device_id={"lat": row - 1}, device_id_type=MESH))
    when(has_above, lambda: pl.semaphore_signal(
        barrier, inc=1, device_id={"lat": row + 1}, device_id_type=MESH))
    inner = jnp.logical_and(has_below, has_above)
    when(inner, lambda: pl.semaphore_wait(barrier, blocks + 1))
    when(jnp.logical_not(inner), lambda: pl.semaphore_wait(barrier, blocks))

    def same_core(t):
        return lax.rem(chip + t, chips)

    def band_copy(slot, target):
        return remote(bands.at[slot], bands.at[slot], band_sems, (target,), (slot,), lon=target)

    def band_mate(slot, landed):
        return remote(bands.at[slot], bands.at[slot], band_mate_sems, (slot,), (landed,), lon=mate)

    def tap_copy(slot, target):
        return remote(all_taps.at[slot], all_taps.at[slot], tap_sems, (target,), (slot,), lon=target)

    bands[me] = band[...]
    all_taps[me] = taps[...]
    loop(1, chips, lambda t: band_copy(me, 2 * same_core(t) + core).start())
    band_mate(me, me).start()
    loop(1, blocks, lambda t: tap_copy(me, lax.rem(me + t, blocks)).start())

    def e_copy(c, target, slot):
        return remote(
            packed.at[target, :, :, at_levels(c)], own_e.at[slot, :, :, at_levels(c)],
            e_sems, (c, target), (c, slot), lon=target)

    def up_copy(c, s):
        return remote(
            own_e.at[s, :, pl.ds(height - half, half), at_levels(c)],
            below_e.at[s, :, :, at_levels(c)], up_sems, (c, s), (c, s), lat=row + 1)

    def down_copy(c, s):
        return remote(
            own_e.at[s, :, pl.ds(0, half), at_levels(c)],
            above_e.at[s, :, :, at_levels(c)], down_sems, (c, s), (c, s), lat=row - 1)

    def pass_on(c, s):
        when(has_above, lambda: up_copy(c, s).start())
        when(has_below, lambda: down_copy(c, s).start())

    def repack(place, target, c):
        for k in range(own):
            value = raw[place * own + k, at_levels(c)].astype(F32)
            turn[k] = value.reshape(GROUP * height, width)
            for y in range(height):
                target[k, y, at_levels(c), :] = turn[
                    k, pl.ds(y, GROUP, stride=height), :].astype(BF16)

    def clear_raw(m):
        for l in range(levels, padded):
            raw[m, l] = jnp.zeros((height, width), BF16)

    loop(0, members, clear_raw)

    def send_near(c):
        load_raw(c, lambda copy: copy.wait())
        repack(mate, packed.at[mate], c)
        e_copy(c, mate, me).start()
        repack(me, own_e.at[me], c)
        pass_on(c, me)

    def send_far(c):
        def other(t):
            p = lax.rem(2 * chip + t, blocks)
            repack(p, packed.at[p], c)
            e_copy(c, p, me).start()

        loop(2, blocks, other)

    def relay(c, s):
        e_copy(c, s, s).wait_recv()
        pass_on(c, s)

    def relay_far(c):
        loop(2, blocks, lambda t: relay(c, lax.rem(2 * chip + t, blocks)))

    loop(0, chunks, send_near)
    loop(0, chunks, send_far)
    loop(0, chunks, lambda c: relay(c, mate))

    edge = (blocks, own, half)
    zero_rows = jnp.zeros((padded, width), BF16)

    def clear_edges(target):
        def clear(b):
            for k in range(own):
                for y in range(half):
                    target[b, k, y] = zero_rows

        loop(0, blocks, clear)

    def clear_facts(first):
        def clear(j):
            for parity in range(2):
                for y in range(half):
                    facts[parity, j, first + y] = zero_rows

        loop(0, chips, clear)

    def clear_sums(target):
        def clear(j):
            for y in range(half):
                target[j, y] = zero_rows

        loop(0, chips, clear)

    def clear_below():
        clear_edges(below_e)
        clear_facts(0)
        clear_sums(below_sums)

    def clear_above():
        clear_edges(above_e)
        clear_facts(height + half)
        clear_sums(above_sums)

    when(jnp.logical_not(has_below), clear_below)
    when(jnp.logical_not(has_above), clear_above)
    inn[pl.ds(rows, padded * height - rows), :] = jnp.zeros((padded * height - rows, width), F32)
    inv[pl.ds(rows, padded * height - rows), :] = jnp.zeros((padded * height - rows, width), F32)

    def clear_tail(b):
        for k in range(own):
            for y in range(height):
                fields[k, y, pl.ds(padded - GROUP, GROUP), lanes(b, width)] = jnp.zeros(
                    (GROUP, width), BF16)

    loop(0, blocks, clear_tail)

    for k in range(own):
        if k > 0:
            relay_far(k - 1)

        def vertical(b):
            load_control(k, b).wait()
            columns = jnp.concatenate(
                [held[b, pl.ds(y, levels, stride=height), :] for y in range(height)], axis=1)
            out = jnp.dot(root[...], columns.astype(BF16), preferred_element_type=F32).astype(BF16)
            for y in range(height):
                fields[k, y, pl.ds(0, levels), lanes(b, width)] = out[:, y * width : (y + 1) * width]
            if k + 1 < own:
                load_control(k + 1, b).start()

        loop(0, blocks, vertical)
        if k == 0:
            def forward_band(t):
                s = 2 * same_core(t) + core
                band_copy(s, s).wait_recv()
                band_mate(s, s).start()

            loop(1, chips, forward_band)
            loop(0, chips, lambda j: band_mate(
                2 * j + 1 - core, 2 * j + 1 - core).wait_recv())
            loop(1, blocks, lambda t: tap_copy(
                lax.rem(me + t, blocks), lax.rem(me + t, blocks)).wait_recv())

        def longitude(b):
            parts = [
                fields[k, :, :, lanes(lax.rem(b + blocks + o, blocks), width)] for o in (-1, 0, 1)]
            left = jnp.concatenate([part.reshape(height * padded, width) for part in parts], axis=1)
            out = jnp.dot(left, bands[b], preferred_element_type=F32)
            spread[b, k] = out.astype(BF16).reshape(height, padded, width)

        loop(0, blocks, longitude)

    def tap_rows(s):
        return [
            jnp.broadcast_to(all_taps[s, pl.ds(o, 1), :], (GROUP, width))
            for o in range(2 * half + 1)]

    def e_row(s, k, r, c):
        if r < half:
            value = below_e[s, k, r, at_levels(c), :]
        elif r < half + height:
            value = own_e[s, k, r - half, at_levels(c), :]
        else:
            value = above_e[s, k, r - half - height, at_levels(c), :]
        return value.astype(F32)

    def stencil(s, c, put):
        tap = tap_rows(s)
        field = [
            [spread[s, k, y, at_levels(c), :].astype(F32) for y in range(height)]
            for k in range(own)]
        for r in range(extended):
            total = None
            for k in range(own):
                part = None
                for o in range(-half, half + 1):
                    y = r - half + o
                    if 0 <= y < height:
                        term = tap[o + half] * field[k][y]
                        part = term if part is None else part + term
                part = part * e_row(s, k, r, c)
                total = part if total is None else total + part
            put(r, total)

    def held_row(j, r, c):
        return 2 * j + r // height, pl.ds(
            pl.multiple_of((r % height) * padded + c * GROUP, GROUP), GROUP)

    def get_held(j, r, c):
        b, at = held_row(j, r, c)
        return held[b, at, :]

    def put_held(j, r, c, value):
        b, at = held_row(j, r, c)
        held[b, at, :] = value

    def core_copy(c, j):
        return remote(sums.at[j, :, at_levels(c)], mate_sums.at[j, :, at_levels(c)],
                      core_sems, (c, j), (c, j), lon=mate)

    def forward(c):
        def other(j):
            for parity in range(2):
                when(has_below, lambda: up_copy(c, 2 * j + parity).wait_recv())
                when(has_above, lambda: down_copy(c, 2 * j + parity).wait_recv())

            def put(r, value):
                sums[j, r, at_levels(c), :] = value.astype(BF16)

            stencil(2 * j + 1 - core, c, put)
            core_copy(c, j).start()

        loop(0, chips, other)
        loop(0, chips, lambda j: stencil(
            2 * j + core, c, lambda r, value: put_held(j, r, c, value)))

    def sum_up(c):
        return remote(sums.at[:, pl.ds(half + height, half), at_levels(c)],
                      below_sums.at[:, :, at_levels(c)], sum_sems, (c, 0), (c, 0), lat=row + 1)

    def sum_down(c):
        return remote(sums.at[:, pl.ds(0, half), at_levels(c)],
                      above_sums.at[:, :, at_levels(c)], sum_sems, (c, 1), (c, 1), lat=row - 1)

    def combine(c):
        def each(j):
            core_copy(c, j).wait()
            for r in range(extended):
                value = get_held(j, r, c) + mate_sums[j, r, at_levels(c), :].astype(F32)
                if half <= r < half + height:
                    put_held(j, r, c, value)
                else:
                    sums[j, r, at_levels(c), :] = value.astype(BF16)

        loop(0, chips, each)
        when(has_above, lambda: sum_up(c).start())
        when(has_below, lambda: sum_down(c).start())

    def lat_sum(j, y, c):
        value = get_held(j, half + y, c)
        if y < half:
            value = value + below_sums[j, y, at_levels(c), :].astype(F32)
        if y >= height - half:
            value = value + above_sums[j, y - height + half, at_levels(c), :].astype(F32)
        return value

    def chip_copy(c, target, slot):
        return remote(sums.at[target, pl.ds(half, height), at_levels(c)],
                      chip_sums.at[slot, :, at_levels(c)],
                      chip_sems, (c, target), (c, slot), lon=2 * target + core)

    def scatter(c):
        when(has_below, lambda: sum_up(c).wait_recv())
        when(has_above, lambda: sum_down(c).wait_recv())

        def each(t):
            j = same_core(t)
            for y in range(height):
                sums[j, half + y, at_levels(c), :] = lat_sum(j, y, c).astype(BF16)
            chip_copy(c, j, chip).start()

        loop(1, chips, each)

    def spread_copy(c, target, slot):
        own_rows = facts.at[core, slot, pl.ds(half, height), at_levels(c)]
        return remote(own_rows, own_rows, spread_sems, (c, target), (c, slot),
                      lon=2 * target + core)

    def depart(c):
        loop(1, chips, lambda t: chip_copy(c, same_core(t), same_core(t)).wait_recv())
        for y in range(height):
            value = lat_sum(chip, y, c)
            for t in range(1, chips):
                value = value + chip_sums[same_core(t), y, at_levels(c), :].astype(F32)
            at = pl.ds(c * GROUP * height + y, GROUP, stride=height)
            value = inv[at, :] * (value - inn[at, :])
            inn[at, :] = value
            facts[core, chip, half + y, at_levels(c), :] = value.astype(BF16)
        loop(1, chips, lambda t: spread_copy(c, same_core(t), chip).start())

    def fact_up(c):
        return remote(facts.at[core, :, pl.ds(height, half), at_levels(c)],
                      facts.at[core, :, pl.ds(0, half), at_levels(c)],
                      fact_sems, (c, 0), (c, 0), lat=row + 1)

    def fact_down(c):
        return remote(facts.at[core, :, pl.ds(half, half), at_levels(c)],
                      facts.at[core, :, pl.ds(half + height, half), at_levels(c)],
                      fact_sems, (c, 1), (c, 1), lat=row - 1)

    def mate_copy(c, part, parity):
        first, count = ((half, height), (0, half), (half + height, half))[part]
        piece = facts.at[parity, :, pl.ds(first, count), at_levels(c)]
        return remote(piece, piece, mate_sems, (c, part), (c, part), lon=mate)

    def gather(c):
        loop(1, chips, lambda t: spread_copy(c, same_core(t), same_core(t)).wait_recv())
        when(has_above, lambda: fact_up(c).start())
        when(has_below, lambda: fact_down(c).start())
        mate_copy(c, 0, core).start()

    def gather_edges(c):
        def below():
            fact_up(c).wait_recv()
            mate_copy(c, 1, core).start()

        def above():
            fact_down(c).wait_recv()
            mate_copy(c, 2, core).start()

        when(has_below, below)
        when(has_above, above)

    def out_copy(g):
        span = together * GROUP
        at = pl.ds(pl.multiple_of(g * span, span), span)
        return pltpu.make_async_copy(
            spread.at[:, :, :, at], summed.at[:, :, :, at], out_sems.at[g])

    def adjoint(c):
        mate_copy(c, 0, 1 - core).wait_recv()
        when(has_below, lambda: mate_copy(c, 1, 1 - core).wait_recv())
        when(has_above, lambda: mate_copy(c, 2, 1 - core).wait_recv())

        def each(s):
            tap = tap_rows(s)
            fact = [facts[lax.rem(s, 2), lax.div(s, 2), r, at_levels(c), :].astype(F32)
                    for r in range(extended)]
            for k in range(own):
                pulled = [e_row(s, k, r, c) * fact[r] for r in range(extended)]
                for y in range(height):
                    total = None
                    for o in range(-half, half + 1):
                        term = tap[o + half] * pulled[y - o + half]
                        total = term if total is None else total + term
                    fields[k, y, at_levels(c), lanes(s, width)] = total.astype(BF16)

        loop(0, blocks, each)

        if together == 1:
            adjoint_longitude(c)
        else:
            when(lax.rem(c, together) == together - 1,
                 lambda: adjoint_longitude(lax.div(c, together)))

    def adjoint_longitude(g):
        span = together * GROUP
        at = pl.ds(pl.multiple_of(g * span, span), span)

        def longitude(b):
            before, after = lax.rem(b + blocks - 1, blocks), lax.rem(b + 1, blocks)
            right = jnp.concatenate(
                [
                    bands[before, 2 * width : 3 * width],
                    bands[b, width : 2 * width],
                    bands[after, 0:width],
                ],
                axis=0,
            )
            left = jnp.concatenate(
                [
                    jnp.concatenate(
                        [fields[k, :, at, lanes(s, width)].reshape(height * span, width)
                         for k in range(own)], axis=0)
                    for s in (before, b, after)
                ],
                axis=1,
            )
            out = jnp.dot(left, right, preferred_element_type=F32).astype(BF16)
            spread[b, :, :, at, :] = out.reshape(own, height, span, width)

        loop(0, blocks, longitude)
        out_copy(g).start()

    def transpose_bands(b):
        for part in range(3):
            at = slice(part * width, (part + 1) * width)
            bands[b, at] = bands[b, at].astype(F32).T.astype(BF16)

    loop(1, chips, lambda t: band_copy(me, 2 * same_core(t) + core).wait_send())
    loop(0, chips, lambda j: band_mate(2 * j + core, 2 * j + core).wait_send())
    loop(0, blocks, transpose_bands)
    load_inn.wait()
    load_inv.wait()

    def stage(action, c):
        when(jnp.logical_and(c >= 0, c < chunks), lambda: action(c))

    def step(i):
        when(i < chunks, lambda: relay_far(i))
        stage(combine, i - OFFSETS[1])
        stage(scatter, i - OFFSETS[2])
        stage(depart, i - OFFSETS[3])
        stage(gather, i - OFFSETS[4])
        stage(gather_edges, i - OFFSETS[5])
        stage(forward, i - OFFSETS[0])
        stage(adjoint, i - OFFSETS[6])

    loop(own - 1, chunks + OFFSETS[6], step)
    store = pltpu.make_async_copy(inn.at[pl.ds(0, rows)], departure, dep_sem)
    store.start()

    def sent(c):
        loop(1, blocks, lambda t: e_copy(c, lax.rem(me + t, blocks), me).wait_send())
        loop(1, chips, lambda t: chip_copy(c, same_core(t), chip).wait_send())
        loop(1, chips, lambda t: spread_copy(c, same_core(t), chip).wait_send())
        mate_copy(c, 0, core).wait_send()

        def below():
            loop(0, blocks, lambda s: down_copy(c, s).wait_send())
            sum_down(c).wait_send()
            fact_down(c).wait_send()
            mate_copy(c, 1, core).wait_send()

        def above():
            loop(0, blocks, lambda s: up_copy(c, s).wait_send())
            sum_up(c).wait_send()
            fact_up(c).wait_send()
            mate_copy(c, 2, core).wait_send()

        when(has_below, below)
        when(has_above, above)

    loop(0, chunks // together, lambda g: out_copy(g).wait())
    loop(0, chunks, sent)
    loop(1, blocks, lambda t: tap_copy(me, lax.rem(me + t, blocks)).wait_send())
    store.wait()


def finish(control, summed, root, departure, gradient, result, held, part, facts, held_sems, part_sems, store_sems, sems):
    levels = root.shape[0]
    blocks, own, height, _, width = summed.shape
    taken = pltpu.make_async_copy(departure, facts, sems.at[0])
    given = pltpu.make_async_copy(facts, result, sems.at[1])

    def place(i):
        return lax.div(i, blocks), lax.rem(i, blocks)

    def load_control(i):
        k, b = place(i)
        return pltpu.make_async_copy(control.at[k, :, lanes(b, width)], held.at[i], held_sems.at[i])

    def load_part(i):
        k, b = place(i)
        return pltpu.make_async_copy(summed.at[b, k], part.at[i], part_sems.at[i])

    def store(i):
        k, b = place(i)
        return pltpu.make_async_copy(held.at[i], gradient.at[k, :, lanes(b, width)], store_sems.at[i])

    def start(i):
        load_part(i).start()
        load_control(i).start()

    def work(i):
        load_part(i).wait()
        right = jnp.concatenate([part[i, y, 0:levels, :] for y in range(height)], axis=1)
        out = lax.dot_general(
            root[...], right, (((0,), (0,)), ((), ())), preferred_element_type=F32)
        out = out.astype(BF16).astype(F32)
        load_control(i).wait()
        for y in range(height):
            at = pl.ds(y, levels, stride=height)
            held[i, at, :] = held[i, at, :] + out[:, y * width : (y + 1) * width]
        store(i).start()

    taken.start()
    loop(0, own * blocks, start)
    taken.wait()
    given.start()
    loop(0, own * blocks, work)
    loop(0, own * blocks, lambda i: store(i).wait())
    given.wait()


def shards(control, ensemble, vertical_root, sector_band, latitude_taps, innovation, inverse_error):
    spans = latitude_taps.shape[0]
    half = spans // 2
    width = sector_band.shape[1]
    own, levels, height, total = control.shape
    members = ensemble.shape[0]
    blocks = total // width
    chips = blocks // 2
    chunks = -(-levels // GROUP)
    padded = chunks * GROUP
    rows = levels * height
    extended = height + 2 * half
    fields = control.reshape(own, rows, total)
    band = sector_band.reshape(3 * width, width)
    dma = pltpu.SemaphoreType.DMA
    vmem = pltpu.VMEM
    local = pl.BlockSpec(memory_space=pltpu.VMEM)
    anywhere = pl.BlockSpec(memory_space=pl.ANY)
    whole = (blocks, own, height, padded, width)
    edges = (blocks, own, half, padded, width)
    summed, departure = pl.pallas_call(
        program,
        in_specs=[anywhere, anywhere, local, local, local, anywhere, anywhere],
        out_specs=[anywhere, anywhere],
        out_shape=[
            jax.ShapeDtypeStruct(whole, BF16),
            jax.ShapeDtypeStruct((rows, width), F32),
        ],
        scratch_shapes=[
            vmem((blocks, height * padded, width), F32),
            vmem((members, padded, height, width), BF16),
            vmem((own, GROUP * height, width), F32),
            vmem(whole, BF16),
            vmem(whole, BF16),
            vmem(edges, BF16),
            vmem(edges, BF16),
            vmem(whole, BF16),
            vmem((own, height, padded, total), BF16),
            vmem((chips, extended, padded, width), BF16),
            vmem((chips, extended, padded, width), BF16),
            vmem((chips, half, padded, width), BF16),
            vmem((chips, half, padded, width), BF16),
            vmem((chips, height, padded, width), BF16),
            vmem((2, chips, extended, padded, width), BF16),
            vmem((padded * height, width), F32),
            vmem((padded * height, width), F32),
            vmem((blocks, 3 * width, width), BF16),
            vmem((blocks, spans, width), F32),
            dma((blocks,)),
            dma((chunks,)),
            dma((2,)),
            dma((chunks,)),
            dma,
            dma((2, chunks, blocks)),
            dma((2, chunks, blocks)),
            dma((2, chunks, blocks)),
            dma((2, chunks, chips)),
            dma((2, chunks, 2)),
            dma((2, chunks, chips)),
            dma((2, chunks, chips)),
            dma((2, chunks, 2)),
            dma((2, chunks, 3)),
            dma((2, blocks)),
            dma((2, blocks)),
            dma((2, blocks)),
        ],
        compiler_params=pltpu.CompilerParams(
            vmem_limit_bytes=VMEM_LIMIT, collective_id=0, has_side_effects=True
        ),
        name="exchange",
    )(fields, ensemble, vertical_root, band, latitude_taps,
      innovation.reshape(rows, width), inverse_error.reshape(rows, width))
    gradient, departure = pl.pallas_call(
        finish,
        in_specs=[anywhere, anywhere, local, anywhere],
        out_specs=[anywhere, anywhere],
        out_shape=[
            jax.ShapeDtypeStruct((own, rows, total), F32),
            jax.ShapeDtypeStruct((rows, width), F32),
        ],
        scratch_shapes=[
            vmem((own * blocks, rows, width), F32),
            vmem((own * blocks, height, padded, width), BF16),
            vmem((rows, width), F32),
            dma((own * blocks,)),
            dma((own * blocks,)),
            dma((own * blocks,)),
            dma((2,)),
        ],
        compiler_params=pltpu.CompilerParams(vmem_limit_bytes=VMEM_LIMIT),
        name="finish",
    )(fields, summed, vertical_root, departure)
    return gradient.reshape(control.shape), departure.reshape(innovation.shape)


def solution(mesh):
    placed = (
        P("lon", None, "lat", None),
        P(None, None, "lat", "lon"),
        P(),
        P(None, None, "lon"),
        P(None, "lon"),
        P(None, "lat", "lon"),
        P(None, "lat", "lon"),
    )
    return jax.shard_map(
        shards,
        mesh=mesh,
        in_specs=placed,
        out_specs=(P("lon", None, "lat", None), P(None, "lat", "lon")),
        check_vma=False,
    )
```
